256 devices in a mesh: event: 8 (over y, core), space: 32 (over x, z).
Axes of the slice: x: 4, y: 4, z: 8, core: 2. Of those that a mesh axis runs over, the one named last changes fastest.
Arguments:
- adjoint_start: float32 [8, 4, 64, 8192], P('event', None, None, 'space'), may hold values from -6 to 6
- checkpoints: bfloat16 [8, 4, 4, 64, 8192], P('event', None, None, None, 'space'), may hold values from -6 to 6
- sound_speed: float32 [64, 8192], P(None, 'space'), may hold values from 0.7 to 1.3
- wind_field: float32 [2, 64, 8192], P(None, None, 'space'), may hold values from -0.4 to 0.4
- neighbours: int32 [6, 8192], P(None, 'space'), may hold values from 0 to 512, as said below
- halo_faces: int32 [2, 4096], P(None, 'space'), may hold values from 0 to 255, as said below
- send_list: int32 [1024, 32], P('space'), may hold values from 0 to 256, as said below
- recv_slots: int32 [1024, 32], P('space'), may hold values from 0 to 256, as said below
- event_source: int32 [8], P('event'), may hold values from 0 to 8191
- source_wave: float32 [8, 64], P('event'), may hold values from -16 to 16
Outputs:
- adjoint_end: float32 [8, 4, 64, 8192], P('event', None, None, 'space')
- speed_gradient: float32 [64, 8192], P(None, 'space')
- wind_gradient: float32 [2, 64, 8192], P(None, None, 'space')
The draws below stay inside these ranges and needn't reach their ends.
Inputs may be any that keep to these rules, and one draw needn't show every extreme that they name: Each device's slab is 2 x 8 x 16 elements stored in a random order, periodic along both horizontal directions (the first across devices) with walls at bottom and top; the lower-side neighbours of a slab's first layer are numbered 256 + 16 * y + z, the upper-side ones 256 + 128 + 16 * y + z, walls 256 + 2 * 128. `halo_faces`: per device, row 0 lists the first layer's elements and row 1 the last layer's, at position 16 * y + z. `send_list`: row s * N + p lists in rising order the old local columns of device s that belong to device p, then 256 in empty slots; every old column is listed once; one peer gets exactly 32; the count depends only on p - s modulo the devices of space. `recv_slots`: row d * N + s gives, slot by slot, the new local column on device d of what row s * N + d of send_list names, 256 in empty slots; each new column occurs once per device.
All inputs are finite; a program needn't handle non-finite values.
Results may differ from the reference program's by a relative error of at most 0.00095.
The reference program's roundings to bfloat16 on the way (of `table_low` and `stored`) count: a program that leaves them out, or rounds other values in their place, can miss the bound.
Values may be sent and summed in bfloat16 or wider, within the bound.
A program may use at most 128 MiB of HBM per device.

```python
import math
import jax
import jax.numpy as jnp
import numpy as np
from jax import lax

EX = 2
EY = 8
EZ = 16
SECTIONS = 4
ELEM_DEV = 256
FACE_ROWS = 128
CAP = 32
NE = 8192
EVENTS = 8
N_SPACE = 32


def mesh_tables(key):
    space_count = NE // ELEM_DEV
    face_rows = EY * EZ
    base = jax.random.fold_in(key, 11)
    orders = jax.vmap(lambda s: jax.random.permutation(jax.random.fold_in(base, s), ELEM_DEV))(jnp.arange(space_count))
    orders = orders.astype(jnp.int32)
    cell_index = jnp.argsort(orders, axis=1).astype(jnp.int32)
    east_place = cell_index // face_rows
    north_place = cell_index // EZ % EY
    up_place = cell_index % EZ

    def slot_of(cells):
        return jnp.take_along_axis(orders, jnp.clip(cells, 0, ELEM_DEV - 1), axis=1)
    side_index = north_place * EZ + up_place
    minus_east = jnp.where(east_place > 0, slot_of(cell_index - face_rows), ELEM_DEV + side_index)
    plus_east = jnp.where(east_place < EX - 1, slot_of(cell_index + face_rows), ELEM_DEV + face_rows + side_index)
    minus_north = slot_of((east_place * EY + (north_place - 1) % EY) * EZ + up_place)
    plus_north = slot_of((east_place * EY + (north_place + 1) % EY) * EZ + up_place)
    minus_up = jnp.where(up_place > 0, slot_of(cell_index - 1), ELEM_DEV + 2 * face_rows)
    plus_up = jnp.where(up_place < EZ - 1, slot_of(cell_index + 1), ELEM_DEV + 2 * face_rows)
    neighbour_table = jnp.stack([minus_east, plus_east, minus_north, plus_north, minus_up, plus_up], axis=0).reshape(6, NE)
    west_faces = orders[:, :face_rows].reshape(-1)
    east_faces = orders[:, (EX - 1) * face_rows:].reshape(-1)
    return (neighbour_table.astype(jnp.int32), jnp.stack([west_faces, east_faces], axis=0).astype(jnp.int32))


def route_tables(key):
    space_count = NE // ELEM_DEV
    base = jax.random.fold_in(key, 23)
    first, second, third = jax.random.split(base, 3)
    heavy = jax.random.randint(first, (), 1, space_count)
    ranking = jnp.argsort(jax.random.permutation(second, ELEM_DEV)).astype(jnp.int32)
    offsets = jnp.where(ranking < CAP, heavy, (heavy + 1 + (ranking - CAP) % (space_count - 1)) % space_count).astype(jnp.int32)
    new_slot = jax.random.permutation(third, ELEM_DEV).astype(jnp.int32)
    column_id = jnp.arange(ELEM_DEV, dtype=jnp.int32)
    ordered = jnp.argsort(offsets * ELEM_DEV + column_id).astype(jnp.int32)
    counts = jnp.sum((offsets[None, :] == jnp.arange(space_count)[:, None]).astype(jnp.int32), axis=1)
    starts = jnp.cumsum(counts) - counts
    slot_id = jnp.arange(CAP, dtype=jnp.int32)
    position = jnp.clip(starts[:, None] + slot_id[None, :], 0, ELEM_DEV - 1)
    lists = jnp.where(slot_id[None, :] < counts[:, None], ordered[position], ELEM_DEV).astype(jnp.int32)
    row_grid = jnp.arange(space_count)[:, None]
    col_grid = jnp.arange(space_count)[None, :]
    send_rows = lists[(col_grid - row_grid) % space_count].reshape(space_count * space_count, CAP)
    incoming = lists[(row_grid - col_grid) % space_count].reshape(space_count * space_count, CAP)
    recv_rows = jnp.where(incoming < ELEM_DEV, new_slot[jnp.clip(incoming, 0, ELEM_DEV - 1)], ELEM_DEV)
    return (send_rows.astype(jnp.int32), recv_rows.astype(jnp.int32))


def draw_neighbours(key, part):
    return mesh_tables(key)[0]


def draw_halo_faces(key, part):
    return mesh_tables(key)[1]


def draw_send_list(key, part):
    return route_tables(key)[0]


def draw_recv_slots(key, part):
    return route_tables(key)[1]


def set_ends(values, key, smallest, top_value):
    longest = values.shape.index(max(values.shape))
    spots = []
    for shift in (0, 1):
        where = [jax.random.randint(jax.random.fold_in(key, axis), (), 0, length) for axis, length in enumerate(values.shape)]
        where[longest] = (where[longest] + shift) % values.shape[longest]
        spots.append(tuple(where))
    return values.at[spots[0]].set(smallest).at[spots[1]].set(top_value)


def block_scale(key, extent, cuts, smallest, largest):
    def one(dim, shards_of):
        heights = jax.random.uniform(jax.random.fold_in(jax.random.fold_in(key, 6), dim), (shards_of,), jnp.float32, smallest / len(cuts), largest / len(cuts))
        return jnp.repeat(jnp.exp(heights), extent[dim] // shards_of).reshape((-1,) + (1,) * (len(extent) - dim - 1))

    factor_of = one(*cuts[0])
    for cut in cuts[1:]:
        factor_of = factor_of * one(*cut)
    return factor_of


def normal_values(stream_key, extent, deviation, reach, cuts=(), held_as=jnp.bfloat16):
    values = deviation * jax.random.normal(stream_key, extent, jnp.float32)
    if cuts:
        values = values * block_scale(stream_key, extent, cuts, -0.22, 0.18)
    return jnp.clip(values, -reach, reach).astype(held_as)


def setup_inputs(seed: int = 0) -> dict:
    arg_keys = jax.random.split(jax.random.key(seed), 11)
    return {
        "adjoint_start": normal_values(arg_keys[0], (EVENTS, 4, 64, NE), 1.0, 6.0, ((0, 8), (3, 32)), jnp.float32),
        "checkpoints": normal_values(arg_keys[1], (EVENTS, SECTIONS, 4, 64, NE), 1.0, 6.0, ((0, 8), (4, 32))),
        "sound_speed": jnp.clip(0.7 + 0.59999996 * jax.random.uniform(arg_keys[2], (64, NE), jnp.float32) ** block_scale(arg_keys[2], (64, NE), ((1, 32),), -0.2, 0.2), 0.7, 1.3),
        "wind_field": jnp.clip(jax.random.uniform(arg_keys[3], (2, 64, NE), jnp.float32, -0.4, 0.4) * block_scale(arg_keys[3], (2, 64, NE), ((2, 32),), -0.4, 0.0), -0.4, 0.4),
        "neighbours": draw_neighbours(jax.random.fold_in(arg_keys[10], 71), 0),
        "halo_faces": draw_halo_faces(jax.random.fold_in(arg_keys[10], 71), 0),
        "send_list": draw_send_list(jax.random.fold_in(arg_keys[10], 71), 0),
        "recv_slots": draw_recv_slots(jax.random.fold_in(arg_keys[10], 71), 0),
        "event_source": set_ends(jax.random.randint(arg_keys[8], (EVENTS,), 0, NE), jax.random.fold_in(arg_keys[8], 1), 0, NE - 1).astype(jnp.int32),
        "source_wave": normal_values(arg_keys[9], (EVENTS, 64), 4.0, 16.0, ((0, 8),), jnp.float32),
    }


HIGHEST_PRECISION = lax.Precision.HIGHEST
TIME_STEP = 0.08
SECTION_SHIFTS = (0.0, 0.04, 0.04, 0.08)
SECTION_WEIGHTS = (0.08 / 6.0, 0.16 / 6.0, 0.16 / 6.0, 0.08 / 6.0)
LIFT_HALF = 3.0

def derivative_table():
    inner_point = 1.0 / math.sqrt(5.0)
    points = np.array([-1.0, -inner_point, inner_point, 1.0])
    products = np.array([np.prod([points[i] - points[k] for k in range(4) if k != i]) for i in range(4)])
    derivative = np.zeros((4, 4))
    for i in range(4):
        for j in range(4):
            if i != j:
                derivative[i, j] = products[i] / (products[j] * (points[i] - points[j]))
            else:
                derivative[i, i] = sum((1.0 / (points[i] - points[k]) for k in range(4) if k != i))
    identity = np.eye(4)
    blocks = [np.kron(derivative, np.kron(identity, identity)), np.kron(identity, np.kron(derivative, identity)), np.kron(identity, np.kron(identity, derivative))]
    return np.concatenate(blocks, axis=0)

def face_trace(values, face_index, leading):
    shaped = values.reshape(values.shape[:leading] + (4, 4, 4, values.shape[-1]))
    position = 0 if face_index % 2 == 0 else 3
    picked = lax.index_in_dim(shaped, position, leading + face_index // 2, keepdims=False)
    return picked.reshape(values.shape[:leading] + (16, values.shape[-1]))

def face_add(values, addition, face_index, leading):
    shaped = values.reshape(values.shape[:leading] + (4, 4, 4, values.shape[-1]))
    position = 0 if face_index % 2 == 0 else 3
    selector = [slice(None)] * shaped.ndim
    selector[leading + face_index // 2] = position
    shaped = shaped.at[tuple(selector)].add(addition.reshape(values.shape[:leading] + (4, 4, values.shape[-1])))
    return shaped.reshape(values.shape)

def acoustic_tendency(field_state, sound_speed, wind_east, wind_north, exterior, source, table):
    derivatives = jnp.einsum('nm,vfme->vfne', table, field_state, precision=HIGHEST_PRECISION)
    derivatives = derivatives.reshape(derivatives.shape[:2] + (3, 64, derivatives.shape[-1]))
    slope_east = derivatives[:, :, 0]
    slope_north = derivatives[:, :, 1]
    slope_up = derivatives[:, :, 2]
    advection = wind_east * slope_east + wind_north * slope_north
    divergence = slope_east[:, 1] + slope_north[:, 2] + slope_up[:, 3]
    tendency = jnp.stack([-advection[:, 0] - sound_speed * sound_speed * divergence + source, -advection[:, 1] - slope_east[:, 0], -advection[:, 2] - slope_north[:, 0], -advection[:, 3] - slope_up[:, 0]], axis=1)
    for face_index in range(6):
        direction = face_index // 2
        normal_sign = -1.0 if face_index % 2 == 0 else 1.0
        face_speed = face_trace(sound_speed, face_index, 0)
        if direction == 0:
            normal_wind = normal_sign * face_trace(wind_east, face_index, 0)
        elif direction == 1:
            normal_wind = normal_sign * face_trace(wind_north, face_index, 0)
        else:
            normal_wind = jnp.zeros_like(face_speed)
        difference = face_trace(field_state, face_index, 2) - exterior[face_index]
        penalty = normal_wind - (face_speed + jnp.abs(normal_wind))
        surface_rows = [penalty * difference[:, 0] + face_speed * face_speed * normal_sign * difference[:, 1 + direction]]
        for component in range(3):
            entry = penalty * difference[:, 1 + component]
            if component == direction:
                entry = entry + normal_sign * difference[:, 0]
            surface_rows.append(entry)
        surface = LIFT_HALF * jnp.stack(surface_rows, axis=1)
        tendency = face_add(tendency, surface, face_index, 2)
    return tendency

def kernel_terms(section_state, stored, sound_speed, table_low):
    slopes = jnp.einsum('nm,vfme->vfne', table_low.astype(jnp.float32), stored.astype(jnp.float32), precision=HIGHEST_PRECISION)
    slopes = slopes.reshape(slopes.shape[:2] + (3, 64, slopes.shape[-1]))
    divergence = slopes[:, 1, 0] + slopes[:, 2, 1] + slopes[:, 3, 2]
    speed_term = lax.optimization_barrier(jnp.sum(section_state[:, 0] * divergence, axis=0)) * (-2.0 * sound_speed)
    east_term = -lax.optimization_barrier(jnp.sum(section_state * slopes[:, :, 0], axis=(0, 1)))
    north_term = -lax.optimization_barrier(jnp.sum(section_state * slopes[:, :, 1], axis=(0, 1)))
    return jnp.stack([speed_term, east_term, north_term], axis=0)

def global_neighbours(neighbours, halo_faces):
    column = jnp.arange(NE, dtype=jnp.int32)
    owner = column // ELEM_DEV
    west_owner = (owner - 1) % N_SPACE
    east_owner = (owner + 1) % N_SPACE
    west_place = jnp.clip(neighbours - ELEM_DEV, 0, FACE_ROWS - 1)
    east_place = jnp.clip(neighbours - ELEM_DEV - FACE_ROWS, 0, FACE_ROWS - 1)
    from_west = west_owner * ELEM_DEV + halo_faces[1][west_owner * FACE_ROWS + west_place]
    from_east = east_owner * ELEM_DEV + halo_faces[0][east_owner * FACE_ROWS + east_place]
    result = jnp.where(neighbours < ELEM_DEV, owner * ELEM_DEV + neighbours, jnp.where(neighbours < ELEM_DEV + FACE_ROWS, from_west, jnp.where(neighbours < ELEM_DEV + 2 * FACE_ROWS, from_east, NE)))
    return result.astype(jnp.int32)

def column_sources(send_list, recv_slots):
    row_id = jnp.arange(N_SPACE * N_SPACE, dtype=jnp.int32)
    sender = row_id // N_SPACE
    peer_id = row_id % N_SPACE
    landing = recv_slots[peer_id * N_SPACE + sender]
    anchor = (sender[:, None] * ELEM_DEV + send_list).astype(jnp.int32)
    target = jnp.where(send_list < ELEM_DEV, peer_id[:, None] * ELEM_DEV + landing, NE).astype(jnp.int32)
    placed = jnp.zeros((NE + 1,), jnp.int32).at[target.reshape(-1)].set(anchor.reshape(-1))
    return placed[:NE]

def exterior_global(field_state, table_global):
    outside = []
    for face_index in range(6):
        face_values = face_trace(field_state, face_index ^ 1, 2)
        padded = jnp.concatenate([face_values, jnp.zeros(face_values.shape[:-1] + (1,), face_values.dtype)], axis=-1)
        outside.append(jnp.take(padded, table_global[face_index], axis=-1))
    return outside

def reference(adjoint_start, checkpoints, sound_speed, wind_field, neighbours, halo_faces, send_list, recv_slots, event_source, source_wave):
    table = jnp.asarray(derivative_table(), jnp.float32)
    table_low = table.astype(jnp.bfloat16)
    table_global = global_neighbours(neighbours, halo_faces)
    old_of_new = column_sources(send_list, recv_slots)
    column = jnp.arange(NE, dtype=jnp.int32)
    wind_east = -wind_field[0]
    wind_north = -wind_field[1]

    def per_event(totals, inputs):
        start, stored, target, wave = inputs
        stored_new = jnp.take(stored, old_of_new, axis=-1)
        source = jnp.where(column[None, None, :] == target, wave[None, :, None], jnp.zeros((), jnp.float32))
        adjoint = start[None]
        section_state = adjoint
        slopes = []
        for section in range(4):
            if section > 0:
                section_state = adjoint + SECTION_SHIFTS[section] * slopes[-1]
            slopes.append(acoustic_tendency(section_state, sound_speed, wind_east, wind_north, exterior_global(section_state, table_global), source, table))
            totals = totals + SECTION_WEIGHTS[section] * kernel_terms(section_state, stored_new[section][None], sound_speed, table_low)
        combined = slopes[0] + 2.0 * slopes[1] + 2.0 * slopes[2] + slopes[3]
        return (totals, (adjoint + TIME_STEP / 6.0 * combined)[0])
    totals, adjoint_end = lax.scan(per_event, jnp.zeros((3, 64, NE), jnp.float32), (adjoint_start, checkpoints, event_source, source_wave))
    return (adjoint_end, totals[0], totals[1:3])
```

```python
import functools
import math

import jax
import jax.numpy as jnp
import numpy as np
from jax import lax
from jax.experimental import pallas as pl
from jax.experimental.pallas import tpu as pltpu
from jax.sharding import PartitionSpec as P

MESH = pl.DeviceIdType.MESH
F32 = jnp.float32
BF16 = jnp.bfloat16
I32 = jnp.int32
TIME_STEP = 0.08
ELEMS = 256
SPACE = 32
EVENTS = 8


def derivative_matrix():
    inner_point = 1.0 / math.sqrt(5.0)
    points = np.array([-1.0, -inner_point, inner_point, 1.0])
    products = np.array(
        [np.prod([points[i] - points[k] for k in range(4) if k != i]) for i in range(4)]
    )
    derivative = np.zeros((4, 4))
    for i in range(4):
        for j in range(4):
            if i != j:
                derivative[i, j] = products[i] / (products[j] * (points[i] - points[j]))
            else:
                derivative[i, i] = sum((1.0 / (points[i] - points[k]) for k in range(4) if k != i))
    return derivative


TABLE = [[float(np.float32(v)) for v in row] for row in derivative_matrix()]
TABLE_LOW = [
    [float(np.float32(jnp.bfloat16(np.float32(v)))) for v in row] for row in derivative_matrix()
]


def iota(shape, dim):
    return lax.broadcasted_iota(I32, shape, dim)


def nn(a, b):
    return lax.dot_general(a, b, (((1,), (0,)), ((), ())), preferred_element_type=F32)


def nt(a, b):
    return lax.dot_general(a, b, (((1,), (1,)), ((), ())), preferred_element_type=F32)


def onehot(condition):
    return jnp.where(condition, 1.0, 0.0).astype(BF16)


def split3(x):
    high = x.astype(BF16)
    rest = x - high.astype(F32)
    middle = rest.astype(BF16)
    low = (rest - middle.astype(F32)).astype(BF16)
    return high, middle, low


def roll(x, shift, axis):
    return pltpu.roll(x, shift % x.shape[axis], axis)


def line(coefficients, pick):
    total = None
    for k in range(4):
        term = coefficients[k] * pick(k)
        total = term if total is None else total + term
    return total


def kernel(
    y_in,
    q_in,
    c_in,
    w_in,
    hf_in,
    sl_in,
    rs_in,
    es_in,
    wave_in,
    out_y,
    out_g,
    states,
    total,
    ge,
    gn,
    gu,
    tend,
    cc,
    w1,
    w2,
    pe,
    pn,
    pu,
    src,
    can,
    can_i,
    halo_send,
    halo_recv,
    sbuf,
    rbuf,
    sbuf2,
    rbuf2,
    qa,
    acc,
    gsend,
    grecv,
    gfull,
    halo_ssem,
    halo_rsem,
    p1_ssem,
    p1_rsem,
    p2_ssem,
    p2_rsem,
    rs_ssem,
    rs_rsem,
    ag_ssem,
    ag_rsem,
):
    me = lax.axis_index("space")
    ev = lax.axis_index("event")
    upper = lax.rem(me + 1, SPACE)
    lower = lax.rem(me + SPACE - 1, SPACE)

    barrier = pltpu.get_barrier_semaphore()

    def greet_space(d, carry):
        pl.semaphore_signal(
            barrier, inc=1, device_id={"space": lax.rem(me + d, SPACE)}, device_id_type=MESH
        )
        return carry

    def greet_event(d, carry):
        pl.semaphore_signal(
            barrier, inc=1, device_id={"event": lax.rem(ev + d, EVENTS)}, device_id_type=MESH
        )
        return carry

    lax.fori_loop(1, SPACE, greet_space, 0)
    lax.fori_loop(1, EVENTS, greet_event, 0)

    wanted = sl_in[...]
    valid = jnp.where(wanted < ELEMS, 1.0, 0.0)
    n_col = jnp.sum(valid, axis=1, keepdims=True)
    n_row = nt(jnp.ones((8, SPACE), BF16), valid.astype(BF16))[0:1]
    offset_rows = jnp.bitwise_and(iota((SPACE, SPACE), 0) + SPACE - me, SPACE - 1)
    offset_cols = jnp.bitwise_and(iota((SPACE, SPACE), 1) + SPACE - me, SPACE - 1)
    back_rows = jnp.bitwise_and(me + SPACE - iota((SPACE, SPACE), 0), SPACE - 1)
    start_col = jnp.sum(jnp.where(offset_cols < offset_rows, n_row, 0.0), axis=1, keepdims=True)
    start_back = jnp.sum(jnp.where(offset_cols < back_rows, n_row, 0.0), axis=1, keepdims=True)
    end_row = jnp.sum(jnp.where(offset_rows <= offset_cols, n_col, 0.0), axis=0, keepdims=True)

    columns = iota((SPACE, ELEMS), 1)
    found = jnp.zeros((SPACE, ELEMS), F32)
    for r in range(SPACE):
        found = found + jnp.where(wanted[:, r : r + 1] == columns, start_col + float(r), 0.0)
    label = jnp.sum(found, axis=0, keepdims=True).astype(I32)
    spot = jnp.bitwise_and(label, 31) * 8 + lax.shift_right_logical(label, 5)
    pick = onehot(iota((ELEMS, ELEMS), 0) == spot)
    halves = [
        nt(pick, q_in[h * 512 : (h + 1) * 512, :]).reshape(SPACE, 8, 512) for h in range(2)
    ]
    sbuf[...] = jnp.concatenate(halves, axis=1).astype(BF16)
    rbuf[me] = sbuf[me]

    pl.semaphore_wait(barrier, SPACE - 1 + EVENTS - 1)

    def phase1(d):
        peer = lax.rem(me + d, SPACE)
        return pltpu.make_async_remote_copy(
            src_ref=sbuf.at[peer],
            dst_ref=rbuf.at[me],
            send_sem=p1_ssem.at[d],
            recv_sem=p1_rsem.at[d],
            device_id={"space": peer},
            device_id_type=MESH,
        )

    def phase2(d):
        peer = lax.rem(me + d, SPACE)
        return pltpu.make_async_remote_copy(
            src_ref=sbuf2.at[peer],
            dst_ref=rbuf2.at[me],
            send_sem=p2_ssem.at[d],
            recv_sem=p2_rsem.at[d],
            device_id={"space": peer},
            device_id_type=MESH,
        )

    def start_all(copy, count):
        def body(d, carry):
            copy(d).start()
            return carry

        lax.fori_loop(1, count, body, 0)

    def wait_all(copy, count):
        def body(d, carry):
            copy(d).wait()
            return carry

        lax.fori_loop(1, count, body, 0)

    start_all(phase1, SPACE)

    hf = hf_in[...]
    hf_row = jnp.concatenate([hf[0:1], hf[1:2]], axis=1)
    can[...] = onehot(iota((ELEMS, ELEMS), 0) == hf_row)
    even = jnp.bitwise_and(iota((1, 8, 128), 1), 1) == 0
    field = lax.shift_right_logical(iota((1, 8, 128), 1), 1)
    height = jnp.bitwise_and(iota((1, 8, 128), 2), 15)

    wide = iota((512, ELEMS), 0)
    spread = onehot(
        iota((512, ELEMS), 1)
        == jnp.bitwise_and(lax.shift_right_logical(wide, 1), 3) * 64
        + lax.shift_right_logical(wide, 3)
    )
    spread_one = onehot(iota((512, 64), 1) == lax.shift_right_logical(iota((512, 64), 0), 3))

    def by_layer(rows):
        return jnp.where(
            even, rows[:, 0:128].reshape(64, 8, 128), rows[:, 128:256].reshape(64, 8, 128)
        )

    def to_slab(x, spreading):
        result = None
        for part in split3(x):
            moved = nn(spreading, nn(part, can[...]).astype(BF16))
            result = moved if result is None else result + moved
        return by_layer(result).reshape(4, 4, 4, 8, 128)

    states[0] = to_slab(y_in[...], spread)
    cc[...] = to_slab(c_in[...], spread_one)
    w1[...] = to_slab(w_in[0:64, :], spread_one)
    w2[...] = to_slab(w_in[64:128, :], spread_one)
    for side, (position, sign) in enumerate(((0, 1.0), (3, -1.0))):
        speed = cc[position]
        wind = sign * w1[position]
        pe[side] = 3.0 * (wind - (speed + jnp.abs(wind)))
        speed = cc[:, position]
        wind = sign * w2[:, position]
        pn[side] = 3.0 * (wind - (speed + jnp.abs(wind)))
        pu[side] = -3.0 * cc[:, :, position]
    cc[...] = jnp.where(field == 0, cc[...] * cc[...], 1.0)
    target = es_in[0] - me * ELEMS
    at_source = (jnp.concatenate([hf, hf, hf, hf], axis=0) == target).reshape(1, 8, 128)
    at_source = jnp.logical_and(at_source, field == 0)[0]

    def place_source(n, carry):
        src[n] = jnp.where(at_source, wave_in[0, n], 0.0)
        return carry

    lax.fori_loop(0, 64, place_source, 0)

    def halo_up(i):
        return pltpu.make_async_remote_copy(
            src_ref=halo_send.at[i, 1],
            dst_ref=halo_recv.at[i, 0],
            send_sem=halo_ssem.at[i, 1],
            recv_sem=halo_rsem.at[i, 0],
            device_id={"space": upper},
            device_id_type=MESH,
        )

    def halo_down(i):
        return pltpu.make_async_remote_copy(
            src_ref=halo_send.at[i, 0],
            dst_ref=halo_recv.at[i, 1],
            send_sem=halo_ssem.at[i, 0],
            recv_sem=halo_rsem.at[i, 1],
            device_id={"space": lower},
            device_id_type=MESH,
        )

    def section(i):
        y = states.at[i]
        first = y[0].reshape(16, 8, 128)
        last = y[3].reshape(16, 8, 128)
        halo_send[i, 1] = (
            jnp.where(even, roll(last[8:16], 7, 1), last[0:8]).reshape(4, 16, 128).astype(BF16)
        )
        halo_send[i, 0] = (
            jnp.where(even, first[0:8], roll(first[8:16], 1, 1)).reshape(4, 16, 128).astype(BF16)
        )
        halo_up(i).start()
        halo_down(i).start()
        for k in range(4):
            ge[k] = line(TABLE[k], lambda j: y[j])
            gn[:, k] = line(TABLE[k], lambda j: y[:, j])
            gu[:, :, k] = line(TABLE[k], lambda j: y[:, :, j])
        tend[...] = w1[...] * ge[...] + w2[...] * gn[...] + src[...].reshape(4, 4, 4, 8, 128)
        for side, (here, there, shift, sign) in enumerate(((0, 3, 16, 3.0), (3, 0, 112, -3.0))):
            outside = roll(y[:, there].reshape(16, 8, 128), shift, 2).reshape(4, 4, 8, 128)
            jump = y[:, here] - outside
            tend[:, here] += pn[side] * jump
            gn[:, here] += sign * jump
        for side, (here, there, shift, sign, wall) in enumerate(
            ((0, 3, 1, 3.0, 0), (3, 0, 127, -3.0, 15))
        ):
            outside = roll(y[:, :, there].reshape(16, 8, 128), shift, 2)
            outside = jnp.where(height == wall, 0.0, outside).reshape(4, 4, 8, 128)
            jump = y[:, :, here] - outside
            tend[:, :, here] += pu[side] * jump
            gu[:, :, here] += sign * jump
        halo_up(i).wait()
        halo_down(i).wait()
        arrived = halo_recv[i, 0].astype(F32).reshape(8, 8, 128)
        arrived = jnp.concatenate([roll(arrived, 7, 1), arrived], axis=0)
        outside = jnp.where(even, arrived, roll(last, 1, 1)).reshape(4, 4, 8, 128)
        jump = y[0] - outside
        tend[0] += pe[0] * jump
        ge[0] += 3.0 * jump
        arrived = halo_recv[i, 1].astype(F32).reshape(8, 8, 128)
        arrived = jnp.concatenate([roll(arrived, 1, 1), arrived], axis=0)
        outside = jnp.where(even, roll(first, 7, 1), arrived).reshape(4, 4, 8, 128)
        jump = y[3] - outside
        tend[3] += pe[1] * jump
        ge[3] += -3.0 * jump
        for a in range(4):
            east = ge[a].reshape(16, 8, 128)
            north = gn[a].reshape(16, 8, 128)
            up = gu[a].reshape(16, 8, 128)
            swapped = (
                roll(jnp.where(field == 0, east, jnp.where(field == 3, up, 0.0)), 2, 1)
                + roll(jnp.where(field == 1, east, jnp.where(field == 0, up, 0.0)), 6, 1)
                + roll(jnp.where(jnp.bitwise_and(field, 1) == 0, north, 0.0), 4, 1)
            )
            slope = tend[a] - cc[a] * swapped.reshape(4, 4, 8, 128)
            if i == 0:
                total[a] = slope
            elif i < 3:
                total[a] += 2.0 * slope
            else:
                total[a] = states[0, a] + (TIME_STEP / 6.0) * (total[a] + slope)
            if i < 3:
                states[i + 1, a] = states[0, a] + (TIME_STEP if i == 2 else TIME_STEP / 2) * slope

    section(0)
    section(1)

    wait_all(phase1, SPACE)
    k8 = iota((8, SPACE), 0) * 32 + me
    off8 = jnp.sum(jnp.where(end_row.astype(I32) <= k8, 1.0, 0.0), axis=1, keepdims=True)
    off = jnp.broadcast_to(off8.astype(I32).reshape(1, 8, 1), (64, 8, 1)).reshape(512, 1)
    row = iota((512, 1), 0)
    origin = (
        jnp.bitwise_and(lax.shift_right_logical(row, 4) - off + SPACE, SPACE - 1) * 16
        + jnp.bitwise_and(row, 15)
    )
    onward = onehot(iota((512, 512), 1) == origin)
    sbuf2[...] = nn(onward, rbuf[...].reshape(512, 512)).astype(BF16).reshape(SPACE, 16, 512)
    rbuf2[me] = sbuf2[me]
    start_all(phase2, SPACE)

    section(2)
    section(3)

    def rows_from_slab(parts, selectors):
        result = None
        for part in parts:
            pieces = [nn(selector, part).astype(BF16) for selector in selectors]
            moved = nt(jnp.concatenate(pieces, axis=1), can[...])
            result = moved if result is None else result + moved
        return result

    shape = (ELEMS, 512)
    wanted_row = (
        jnp.bitwise_and(iota(shape, 0), 63) * 8 + lax.shift_right_logical(iota(shape, 0), 6) * 2
    )
    gather_rows = [onehot(iota(shape, 1) == wanted_row + layer) for layer in range(2)]
    out_y[...] = rows_from_slab(split3(total[...].reshape(512, 128)), gather_rows)

    landing = rs_in[...]
    places = iota((SPACE, 512), 1)
    landed = jnp.zeros((SPACE, 512), F32)
    for r in range(SPACE):
        label = start_back.astype(I32) + r
        place = jnp.bitwise_and(label, 31) * 16 + lax.shift_right_logical(label, 5)
        column = landing[:, r : r + 1]
        hit = jnp.logical_and(places == place, column < ELEMS)
        landed = landed + jnp.where(hit, column.astype(F32) + 1.0, 0.0)
    land_row = jnp.sum(landed, axis=0, keepdims=True) - 1.0
    land_row = jnp.broadcast_to(land_row, (8, 512))
    eye = onehot(iota((ELEMS, ELEMS), 0) == iota((ELEMS, ELEMS), 1))
    hf_col = nt(eye, jnp.broadcast_to(hf_row, (8, ELEMS)).astype(F32).astype(BF16))[:, 0:1]

    wait_all(phase2, SPACE)
    for h in range(2):
        place_row = (land_row if h == 0 else roll(land_row, 8, 1))[0:1]
        settle = onehot(hf_col == place_row)
        settled = nn(settle, rbuf2[...].reshape(512, 512)).astype(BF16)
        for part in range(2):
            rows = nt(spread, settled[:, part * 256 : (part + 1) * 256])
            qa[2 * h + part] = by_layer(rows).reshape(4, 4, 4, 8, 128)

    weights = [TIME_STEP / 6.0, TIME_STEP / 3.0, TIME_STEP / 3.0, TIME_STEP / 6.0]
    for a in range(4):
        east = north = speed = None
        for i in range(4):
            q = qa.at[i]
            d_east = line(TABLE_LOW[a], lambda j: q[j]).reshape(16, 8, 128)
            d_north = jnp.stack(
                [line(TABLE_LOW[k], lambda j: q[a, j]) for k in range(4)], axis=0
            ).reshape(16, 8, 128)
            d_up = jnp.stack(
                [line(TABLE_LOW[k], lambda j: q[a, :, j]) for k in range(4)], axis=1
            ).reshape(16, 8, 128)
            y = weights[i] * states[i, a].reshape(16, 8, 128)
            own = jnp.where(field == 0, y, 0.0)
            own = own + roll(own, 4, 1)
            own = own + roll(own, 2, 1)
            part = own * jnp.where(
                field == 1,
                d_east,
                jnp.where(field == 2, d_north, jnp.where(field == 3, d_up, 0.0)),
            )
            east = y * d_east if east is None else east + y * d_east
            north = y * d_north if north is None else north + y * d_north
            speed = part if speed is None else speed + part
        acc[0, a * 16 : (a + 1) * 16] = speed
        acc[1, a * 16 : (a + 1) * 16] = east
        acc[2, a * 16 : (a + 1) * 16] = north
    for g in range(3):
        sums = acc[g] + roll(acc[g], 4, 1)
        sums = (sums + roll(sums, 2, 1)).reshape(16, 4, 8, 128)
        packed = jnp.where(
            field == 0,
            sums[:, 0],
            jnp.where(field == 1, sums[:, 1], jnp.where(field == 2, sums[:, 2], sums[:, 3])),
        )
        gsend[:, g] = (-packed).reshape(EVENTS, 2, 8, 128)

    def scatter(d):
        peer = lax.rem(ev + d, EVENTS)
        return pltpu.make_async_remote_copy(
            src_ref=gsend.at[peer],
            dst_ref=grecv.at[ev],
            send_sem=rs_ssem.at[d],
            recv_sem=rs_rsem.at[d],
            device_id={"event": peer},
            device_id_type=MESH,
        )

    def gather(d):
        peer = lax.rem(ev + d, EVENTS)
        return pltpu.make_async_remote_copy(
            src_ref=gfull.at[ev],
            dst_ref=gfull.at[ev],
            send_sem=ag_ssem.at[d],
            recv_sem=ag_rsem.at[d],
            device_id={"event": peer},
            device_id_type=MESH,
        )

    grecv[ev] = gsend[ev]
    start_all(scatter, EVENTS)
    shape = (192, 384)
    q_row = iota(shape, 0)
    node = jnp.bitwise_and(q_row, 63)
    group = lax.shift_right_logical(node, 2)
    position = (
        lax.shift_right_logical(group, 1) * 48
        + lax.shift_right_logical(q_row, 6) * 16
        + jnp.bitwise_and(group, 1) * 8
        + jnp.bitwise_and(node, 3) * 2
    )
    gather_rows = [onehot(iota(shape, 1) == position + layer) for layer in range(2)]
    wait_all(scatter, EVENTS)
    summed = grecv[0]
    for e in range(1, EVENTS):
        summed = summed + grecv[e]
    gfull[ev] = summed
    start_all(gather, EVENTS)
    wait_all(gather, EVENTS)
    result = rows_from_slab(split3(gfull[...].reshape(384, 128)), gather_rows)
    out_g[0:64, :] = 2.0 * c_in[...] * result[0:64, :]
    out_g[64:192, :] = result[64:192, :]


def shards(
    adjoint_start,
    checkpoints,
    sound_speed,
    wind_field,
    neighbours,
    halo_faces,
    send_list,
    recv_slots,
    event_source,
    source_wave,
):
    del neighbours
    vmem = pl.BlockSpec(memory_space=pltpu.VMEM)
    smem = pl.BlockSpec(memory_space=pltpu.SMEM)
    nodes = (4, 4, 4, 8, 128)
    dma = pltpu.SemaphoreType.DMA
    end, gradients = pl.pallas_call(
        kernel,
        out_shape=(
            jax.ShapeDtypeStruct((ELEMS, ELEMS), F32),
            jax.ShapeDtypeStruct((192, ELEMS), F32),
        ),
        in_specs=[vmem] * 7 + [smem] * 2,
        out_specs=(vmem, vmem),
        scratch_shapes=[
            pltpu.VMEM((4,) + nodes, F32),
            pltpu.VMEM(nodes, F32),
            pltpu.VMEM(nodes, F32),
            pltpu.VMEM(nodes, F32),
            pltpu.VMEM(nodes, F32),
            pltpu.VMEM(nodes, F32),
            pltpu.VMEM(nodes, F32),
            pltpu.VMEM(nodes, F32),
            pltpu.VMEM(nodes, F32),
            pltpu.VMEM((2, 4, 4, 8, 128), F32),
            pltpu.VMEM((2, 4, 4, 8, 128), F32),
            pltpu.VMEM((2, 4, 4, 8, 128), F32),
            pltpu.VMEM((64, 8, 128), F32),
            pltpu.VMEM((ELEMS, ELEMS), BF16),
            pltpu.VMEM((8, 128), F32),
            pltpu.VMEM((4, 2, 4, 16, 128), BF16),
            pltpu.VMEM((4, 2, 4, 16, 128), BF16),
            pltpu.VMEM((SPACE, 16, 512), BF16),
            pltpu.VMEM((SPACE, 16, 512), BF16),
            pltpu.VMEM((SPACE, 16, 512), BF16),
            pltpu.VMEM((SPACE, 16, 512), BF16),
            pltpu.VMEM((4,) + nodes, F32),
            pltpu.VMEM((3, 64, 8, 128), F32),
            pltpu.VMEM((EVENTS, 3, 2, 8, 128), F32),
            pltpu.VMEM((EVENTS, 3, 2, 8, 128), F32),
            pltpu.VMEM((EVENTS, 3, 2, 8, 128), F32),
            dma((4, 2)),
            dma((4, 2)),
            dma((SPACE,)),
            dma((SPACE,)),
            dma((SPACE,)),
            dma((SPACE,)),
            dma((EVENTS,)),
            dma((EVENTS,)),
            dma((EVENTS,)),
            dma((EVENTS,)),
        ],
        compiler_params=pltpu.CompilerParams(
            collective_id=0, has_side_effects=True, vmem_limit_bytes=48 * 1024 * 1024
        ),
        name="adjoint_step",
    )(
        adjoint_start.reshape(ELEMS, ELEMS),
        checkpoints.reshape(1024, ELEMS),
        sound_speed,
        wind_field.reshape(128, ELEMS),
        halo_faces,
        send_list,
        recv_slots,
        event_source,
        source_wave,
    )
    return (
        end.reshape(1, 4, 64, ELEMS),
        gradients[0:64],
        gradients[64:192].reshape(2, 64, ELEMS),
    )


def solution(mesh):
    return jax.shard_map(
        shards,
        mesh=mesh,
        in_specs=(
            P("event", None, None, "space"),
            P("event", None, None, None, "space"),
            P(None, "space"),
            P(None, None, "space"),
            P(None, "space"),
            P(None, "space"),
            P("space", None),
            P("space", None),
            P("event"),
            P("event", None),
        ),
        out_specs=(P("event", None, None, "space"), P(None, "space"), P(None, None, "space")),
        check_vma=False,
    )
```

```python
import functools
import math

import jax
import jax.numpy as jnp
import numpy as np
from jax import lax
from jax.experimental import pallas as pl
from jax.experimental.pallas import tpu as pltpu
from jax.sharding import PartitionSpec as P

MESH = pl.DeviceIdType.MESH
F32 = jnp.float32
BF16 = jnp.bfloat16
I32 = jnp.int32
TIME_STEP = 0.08
ELEMS = 256
SPACE = 32
EVENTS = 8


def derivative_matrix():
    inner_point = 1.0 / math.sqrt(5.0)
    points = np.array([-1.0, -inner_point, inner_point, 1.0])
    products = np.array(
        [np.prod([points[i] - points[k] for k in range(4) if k != i]) for i in range(4)]
    )
    derivative = np.zeros((4, 4))
    for i in range(4):
        for j in range(4):
            if i != j:
                derivative[i, j] = products[i] / (products[j] * (points[i] - points[j]))
            else:
                derivative[i, i] = sum((1.0 / (points[i] - points[k]) for k in range(4) if k != i))
    return derivative


TABLE = [[float(np.float32(v)) for v in row] for row in derivative_matrix()]
TABLE_LOW = [
    [float(np.float32(jnp.bfloat16(np.float32(v)))) for v in row] for row in derivative_matrix()
]


def iota(shape, dim):
    return lax.broadcasted_iota(I32, shape, dim)


def nn(a, b):
    return lax.dot_general(a, b, (((1,), (0,)), ((), ())), preferred_element_type=F32)


def nt(a, b):
    return lax.dot_general(a, b, (((1,), (1,)), ((), ())), preferred_element_type=F32)


def onehot(condition):
    return jnp.where(condition, 1.0, 0.0).astype(BF16)


def split3(x):
    high = x.astype(BF16)
    rest = x - high.astype(F32)
    middle = rest.astype(BF16)
    low = (rest - middle.astype(F32)).astype(BF16)
    return high, middle, low


def roll(x, shift, axis):
    return pltpu.roll(x, shift % x.shape[axis], axis)


def line(coefficients, pick):
    total = None
    for k in range(4):
        term = coefficients[k] * pick(k)
        total = term if total is None else total + term
    return total


def kernel(
    y_hbm,
    q_hbm,
    c_hbm,
    w_hbm,
    hf_hbm,
    sl_hbm,
    rs_hbm,
    es_hbm,
    wave_hbm,
    out_y,
    out_s,
    out_w,
    y_in,
    q_in,
    c_in,
    w_in,
    hf_in,
    sl_in,
    rs_in,
    es_in,
    wave_in,
    states,
    total,
    ge,
    gn,
    gu,
    tend,
    cc,
    w1,
    w2,
    pe,
    pn,
    pu,
    src,
    can,
    spread,
    onward,
    settle,
    halo_send,
    halo_recv,
    sbuf,
    rbuf,
    sbuf2,
    rbuf2,
    qa,
    acc,
    gsend,
    grecv,
    gfull,
    in_sem,
    halo_ssem,
    halo_rsem,
    p1_ssem,
    p1_rsem,
    p2_ssem,
    p2_rsem,
    rs_ssem,
    rs_rsem,
    ag_ssem,
    ag_rsem,
):
    me = lax.axis_index("space")
    ev = lax.axis_index("event")
    upper = lax.rem(me + 1, SPACE)
    lower = lax.rem(me + SPACE - 1, SPACE)

    inputs = (
        (sl_hbm, sl_in),
        (q_hbm, q_in),
        (hf_hbm, hf_in),
        (y_hbm, y_in),
        (c_hbm, c_in),
        (w_hbm, w_in),
        (rs_hbm, rs_in),
        (es_hbm, es_in),
        (wave_hbm, wave_in),
    )
    fetches = [
        pltpu.make_async_copy(source, target, in_sem.at[k])
        for k, (source, target) in enumerate(inputs)
    ]
    for fetch in fetches:
        fetch.start()

    barrier = pltpu.get_barrier_semaphore()

    def greet_space(d, carry):
        pl.semaphore_signal(
            barrier, inc=1, device_id={"space": lax.rem(me + d, SPACE)}, device_id_type=MESH
        )
        return carry

    def greet_event(d, carry):
        pl.semaphore_signal(
            barrier, inc=1, device_id={"event": lax.rem(ev + d, EVENTS)}, device_id_type=MESH
        )
        return carry

    lax.fori_loop(1, SPACE, greet_space, 0)
    lax.fori_loop(1, EVENTS, greet_event, 0)

    fetches[0].wait()
    wanted = sl_in[...]
    valid = jnp.where(wanted < ELEMS, 1.0, 0.0)
    n_col = jnp.sum(valid, axis=1, keepdims=True)
    n_row = nt(jnp.ones((8, SPACE), BF16), valid.astype(BF16))[0:1]
    offset_rows = jnp.bitwise_and(iota((SPACE, SPACE), 0) + SPACE - me, SPACE - 1)
    offset_cols = jnp.bitwise_and(iota((SPACE, SPACE), 1) + SPACE - me, SPACE - 1)
    back_rows = jnp.bitwise_and(me + SPACE - iota((SPACE, SPACE), 0), SPACE - 1)
    start_col = jnp.sum(jnp.where(offset_cols < offset_rows, n_row, 0.0), axis=1, keepdims=True)
    start_back = jnp.sum(jnp.where(offset_cols < back_rows, n_row, 0.0), axis=1, keepdims=True)
    end_row = jnp.sum(jnp.where(offset_rows <= offset_cols, n_col, 0.0), axis=0, keepdims=True)

    columns = iota((SPACE, ELEMS), 1)
    found = jnp.zeros((SPACE, ELEMS), F32)
    for r in range(SPACE):
        found = found + jnp.where(wanted[:, r : r + 1] == columns, start_col + float(r), 0.0)
    label = jnp.sum(found, axis=0, keepdims=True).astype(I32)
    spot = jnp.bitwise_and(label, 31) * 8 + lax.shift_right_logical(label, 5)
    pick = onehot(iota((ELEMS, ELEMS), 0) == spot)
    fetches[1].wait()

    def fill(part):
        pieces = [
            nt(pick, q_in[h * 512 + part * 256 : h * 512 + part * 256 + 256, :])
            for h in range(2)
        ]
        pieces = [piece.reshape(SPACE, 8, 256) for piece in pieces]
        sbuf[part] = jnp.concatenate(pieces, axis=1).astype(BF16)
        rbuf[part, me] = sbuf[part, me]

    def phase1(part):
        def copy(d):
            peer = lax.rem(me + d, SPACE)
            return pltpu.make_async_remote_copy(
                src_ref=sbuf.at[part, peer],
                dst_ref=rbuf.at[part, me],
                send_sem=p1_ssem.at[part, d],
                recv_sem=p1_rsem.at[part, d],
                device_id={"space": peer},
                device_id_type=MESH,
            )

        return copy

    def phase2(part):
        def copy(d):
            peer = lax.rem(me + d, SPACE)
            return pltpu.make_async_remote_copy(
                src_ref=sbuf2.at[part, peer],
                dst_ref=rbuf2.at[part, me],
                send_sem=p2_ssem.at[part, d],
                recv_sem=p2_rsem.at[part, d],
                device_id={"space": peer},
                device_id_type=MESH,
            )

        return copy

    def start_all(copy, count):
        def body(d, carry):
            copy(d).start()
            return carry

        lax.fori_loop(1, count, body, 0)

    def wait_all(copy, count):
        def body(d, carry):
            copy(d).wait_recv()
            return carry

        lax.fori_loop(1, count, body, 0)

    def finish_all(copy, count):
        def body(d, carry):
            copy(d).wait_send()
            return carry

        lax.fori_loop(1, count, body, 0)

    fill(0)
    pl.semaphore_wait(barrier, SPACE - 1 + EVENTS - 1)
    start_all(phase1(0), SPACE)
    fill(1)

    for fetch in fetches[2:]:
        fetch.wait()
    hf = hf_in[...]
    hf_row = jnp.concatenate([hf[0:1], hf[1:2]], axis=1)
    can[...] = onehot(iota((ELEMS, ELEMS), 0) == hf_row)
    even = jnp.bitwise_and(iota((1, 8, 128), 1), 1) == 0
    field = lax.shift_right_logical(iota((1, 8, 128), 1), 1)
    height = jnp.bitwise_and(iota((1, 8, 128), 2), 15)

    wide = iota((512, ELEMS), 0)
    spread[...] = onehot(
        iota((512, ELEMS), 1)
        == jnp.bitwise_and(lax.shift_right_logical(wide, 1), 3) * 64
        + lax.shift_right_logical(wide, 3)
    )
    spread_one = onehot(iota((512, 64), 1) == lax.shift_right_logical(iota((512, 64), 0), 3))

    def by_layer(rows):
        return jnp.where(
            even, rows[:, 0:128].reshape(64, 8, 128), rows[:, 128:256].reshape(64, 8, 128)
        )

    def to_slab(x, spreading):
        result = None
        for part in split3(x):
            moved = nn(spreading, nn(part, can[...]).astype(BF16))
            result = moved if result is None else result + moved
        return by_layer(result).reshape(4, 4, 4, 8, 128)

    states[0] = to_slab(y_in[...], spread[...])
    cc[...] = to_slab(c_in[...], spread_one)
    w1[...] = to_slab(w_in[0:64, :], spread_one)
    w2[...] = to_slab(w_in[64:128, :], spread_one)
    for side, (position, sign) in enumerate(((0, 1.0), (3, -1.0))):
        speed = cc[position]
        wind = sign * w1[position]
        pe[side] = 3.0 * (wind - (speed + jnp.abs(wind)))
        speed = cc[:, position]
        wind = sign * w2[:, position]
        pn[side] = 3.0 * (wind - (speed + jnp.abs(wind)))
        pu[side] = -3.0 * cc[:, :, position]
    cc[...] = jnp.where(field == 0, cc[...] * cc[...], 1.0)
    target = es_in[0] - me * ELEMS
    at_source = (jnp.concatenate([hf, hf, hf, hf], axis=0) == target).reshape(1, 8, 128)
    at_source = jnp.logical_and(at_source, field == 0)[0]

    def place_source(n, carry):
        src[n] = jnp.where(at_source, wave_in[0, n], 0.0)
        return carry

    lax.fori_loop(0, 64, place_source, 0)

    def halo_up(i):
        return pltpu.make_async_remote_copy(
            src_ref=halo_send.at[i, 1],
            dst_ref=halo_recv.at[i, 0],
            send_sem=halo_ssem.at[i, 1],
            recv_sem=halo_rsem.at[i, 0],
            device_id={"space": upper},
            device_id_type=MESH,
        )

    def halo_down(i):
        return pltpu.make_async_remote_copy(
            src_ref=halo_send.at[i, 0],
            dst_ref=halo_recv.at[i, 1],
            send_sem=halo_ssem.at[i, 0],
            recv_sem=halo_rsem.at[i, 1],
            device_id={"space": lower},
            device_id_type=MESH,
        )

    def send_halo(i):
        first = states[i, 0].reshape(16, 8, 128)
        last = states[i, 3].reshape(16, 8, 128)
        halo_send[i, 1] = (
            jnp.where(even, roll(last[8:16], 7, 1), last[0:8]).reshape(4, 16, 128).astype(BF16)
        )
        halo_send[i, 0] = (
            jnp.where(even, first[0:8], roll(first[8:16], 1, 1)).reshape(4, 16, 128).astype(BF16)
        )
        halo_up(i).start()
        halo_down(i).start()

    def section(i):
        y = states.at[i]
        first = y[0].reshape(16, 8, 128)
        last = y[3].reshape(16, 8, 128)
        for k in range(4):
            ge[k] = line(TABLE[k], lambda j: y[j])
            gn[:, k] = line(TABLE[k], lambda j: y[:, j])
            gu[:, :, k] = line(TABLE[k], lambda j: y[:, :, j])
        tend[...] = w1[...] * ge[...] + w2[...] * gn[...] + src[...].reshape(4, 4, 4, 8, 128)
        for side, (here, there, shift, sign) in enumerate(((0, 3, 16, 3.0), (3, 0, 112, -3.0))):
            outside = roll(y[:, there].reshape(16, 8, 128), shift, 2).reshape(4, 4, 8, 128)
            jump = y[:, here] - outside
            tend[:, here] += pn[side] * jump
            gn[:, here] += sign * jump
        for side, (here, there, shift, sign, wall) in enumerate(
            ((0, 3, 1, 3.0, 0), (3, 0, 127, -3.0, 15))
        ):
            outside = roll(y[:, :, there].reshape(16, 8, 128), shift, 2)
            outside = jnp.where(height == wall, 0.0, outside).reshape(4, 4, 8, 128)
            jump = y[:, :, here] - outside
            tend[:, :, here] += pu[side] * jump
            gu[:, :, here] += sign * jump
        halo_up(i).wait_recv()
        halo_down(i).wait_recv()
        arrived = halo_recv[i, 0].astype(F32).reshape(8, 8, 128)
        arrived = jnp.concatenate([roll(arrived, 7, 1), arrived], axis=0)
        outside = jnp.where(even, arrived, roll(last, 1, 1)).reshape(4, 4, 8, 128)
        jump = y[0] - outside
        tend[0] += pe[0] * jump
        ge[0] += 3.0 * jump
        arrived = halo_recv[i, 1].astype(F32).reshape(8, 8, 128)
        arrived = jnp.concatenate([roll(arrived, 1, 1), arrived], axis=0)
        outside = jnp.where(even, roll(first, 7, 1), arrived).reshape(4, 4, 8, 128)
        jump = y[3] - outside
        tend[3] += pe[1] * jump
        ge[3] += -3.0 * jump
        for a in range(4):
            east = ge[a].reshape(16, 8, 128)
            north = gn[a].reshape(16, 8, 128)
            up = gu[a].reshape(16, 8, 128)
            swapped = (
                roll(jnp.where(field == 0, east, jnp.where(field == 3, up, 0.0)), 2, 1)
                + roll(jnp.where(field == 1, east, jnp.where(field == 0, up, 0.0)), 6, 1)
                + roll(jnp.where(jnp.bitwise_and(field, 1) == 0, north, 0.0), 4, 1)
            )
            slope = tend[a] - cc[a] * swapped.reshape(4, 4, 8, 128)
            if i == 0:
                total[a] = slope
            elif i < 3:
                total[a] += 2.0 * slope
            else:
                total[a] = states[0, a] + (TIME_STEP / 6.0) * (total[a] + slope)
            if i < 3:
                states[i + 1, a] = states[0, a] + (TIME_STEP if i == 2 else TIME_STEP / 2) * slope

    k8 = iota((8, SPACE), 0) * 32 + me
    off8 = jnp.sum(jnp.where(end_row.astype(I32) <= k8, 1.0, 0.0), axis=1, keepdims=True)
    off = jnp.broadcast_to(off8.astype(I32).reshape(1, 8, 1), (64, 8, 1)).reshape(512, 1)
    row = iota((512, 1), 0)
    origin = (
        jnp.bitwise_and(lax.shift_right_logical(row, 4) - off + SPACE, SPACE - 1) * 16
        + jnp.bitwise_and(row, 15)
    )

    def relay(part):
        wait_all(phase1(part), SPACE)
        rows = nn(onward[...], rbuf[part].reshape(512, 256)).astype(BF16)
        sbuf2[part] = rows.reshape(SPACE, 16, 256)
        rbuf2[part, me] = sbuf2[part, me]
        start_all(phase2(part), SPACE)

    send_halo(0)
    start_all(phase1(1), SPACE)
    onward[...] = onehot(iota((512, 512), 1) == origin)
    section(0)
    send_halo(1)
    relay(0)
    section(1)
    send_halo(2)
    relay(1)
    section(2)
    send_halo(3)

    def rows_from_slab(parts, selectors):
        result = None
        for part in parts:
            pieces = [nn(selector, part).astype(BF16) for selector in selectors]
            moved = nt(jnp.concatenate(pieces, axis=1), can[...])
            result = moved if result is None else result + moved
        return result

    shape = (ELEMS, 512)
    wanted_row = (
        jnp.bitwise_and(iota(shape, 0), 63) * 8 + lax.shift_right_logical(iota(shape, 0), 6) * 2
    )
    gather_rows = [onehot(iota(shape, 1) == wanted_row + layer) for layer in range(2)]
    landing = rs_in[...]
    places = iota((SPACE, 512), 1)
    landed = jnp.zeros((SPACE, 512), F32)
    for r in range(SPACE):
        label = start_back.astype(I32) + r
        place = jnp.bitwise_and(label, 31) * 16 + lax.shift_right_logical(label, 5)
        column = landing[:, r : r + 1]
        hit = jnp.logical_and(places == place, column < ELEMS)
        landed = landed + jnp.where(hit, column.astype(F32) + 1.0, 0.0)
    land_row = jnp.sum(landed, axis=0, keepdims=True) - 1.0
    land_row = jnp.broadcast_to(land_row, (8, 512))
    eye = onehot(iota((ELEMS, ELEMS), 0) == iota((ELEMS, ELEMS), 1))
    hf_col = nt(eye, jnp.broadcast_to(hf_row, (8, ELEMS)).astype(F32).astype(BF16))[:, 0:1]

    for h in range(2):
        place_row = (land_row if h == 0 else roll(land_row, 8, 1))[0:1]
        settle[h] = onehot(hf_col == place_row)

    weights = [TIME_STEP / 6.0, TIME_STEP / 3.0, TIME_STEP / 3.0, TIME_STEP / 6.0]
    for part in range(2):
        wait_all(phase2(part), SPACE)
        for h in range(2):
            settled = nn(settle[h], rbuf2[part].reshape(512, 256)).astype(BF16)
            qa[h] = by_layer(nt(spread[...], settled)).reshape(4, 4, 4, 8, 128)
        for a in range(4):
            east = north = speed = None
            for h in range(2):
                i = 2 * h + part
                q = qa.at[h]
                d_east = line(TABLE_LOW[a], lambda j: q[j]).reshape(16, 8, 128)
                d_north = jnp.stack(
                    [line(TABLE_LOW[k], lambda j: q[a, j]) for k in range(4)], axis=0
                ).reshape(16, 8, 128)
                d_up = jnp.stack(
                    [line(TABLE_LOW[k], lambda j: q[a, :, j]) for k in range(4)], axis=1
                ).reshape(16, 8, 128)
                y = weights[i] * states[i, a].reshape(16, 8, 128)
                own = jnp.where(field == 0, y, 0.0)
                own = own + roll(own, 4, 1)
                own = own + roll(own, 2, 1)
                product = own * jnp.where(
                    field == 1,
                    d_east,
                    jnp.where(field == 2, d_north, jnp.where(field == 3, d_up, 0.0)),
                )
                east = y * d_east if east is None else east + y * d_east
                north = y * d_north if north is None else north + y * d_north
                speed = product if speed is None else speed + product
            rows = slice(a * 16, (a + 1) * 16)
            if part == 0:
                acc[0, rows] = speed
                acc[1, rows] = east
                acc[2, rows] = north
            else:
                acc[0, rows] += speed
                acc[1, rows] += east
                acc[2, rows] += north
    for g in range(3):
        sums = acc[g] + roll(acc[g], 4, 1)
        sums = (sums + roll(sums, 2, 1)).reshape(16, 4, 8, 128)
        packed = jnp.where(
            field == 0,
            sums[:, 0],
            jnp.where(field == 1, sums[:, 1], jnp.where(field == 2, sums[:, 2], sums[:, 3])),
        )
        gsend[:, g] = (-packed).reshape(EVENTS, 2, 8, 128)

    def scatter(d):
        peer = lax.rem(ev + d, EVENTS)
        return pltpu.make_async_remote_copy(
            src_ref=gsend.at[peer],
            dst_ref=grecv.at[ev],
            send_sem=rs_ssem.at[d],
            recv_sem=rs_rsem.at[d],
            device_id={"event": peer},
            device_id_type=MESH,
        )

    def gather(d):
        peer = lax.rem(ev + d, EVENTS)
        return pltpu.make_async_remote_copy(
            src_ref=gfull.at[ev],
            dst_ref=gfull.at[ev],
            send_sem=ag_ssem.at[d],
            recv_sem=ag_rsem.at[d],
            device_id={"event": peer},
            device_id_type=MESH,
        )

    grecv[ev] = gsend[ev]
    start_all(scatter, EVENTS)
    section(3)
    out_y[...] = rows_from_slab(split3(total[...].reshape(512, 128)), gather_rows)
    shape = (24, 48)
    node = jnp.bitwise_and(iota(shape, 0), 7)
    position = (
        lax.shift_right_logical(iota(shape, 0), 3) * 16
        + lax.shift_right_logical(node, 2) * 8
        + jnp.bitwise_and(node, 3) * 2
    )
    gather_rows = [onehot(iota(shape, 1) == position + layer) for layer in range(2)]
    wait_all(scatter, EVENTS)
    summed = grecv[0]
    for e in range(1, EVENTS):
        summed = summed + grecv[e]
    rows = rows_from_slab(split3(summed.reshape(48, 128)), gather_rows)
    speed = c_in[pl.ds(pl.multiple_of(ev * 8, 8), 8), :]
    gfull[ev] = jnp.concatenate([2.0 * speed * rows[0:8], rows[8:24]], axis=0).reshape(3, 8, ELEMS)
    start_all(gather, EVENTS)
    wait_all(gather, EVENTS)
    for e in range(EVENTS):
        out_s[e * 8 : (e + 1) * 8, :] = gfull[e, 0]
        out_w[e * 8 : (e + 1) * 8, :] = gfull[e, 1]
        out_w[64 + e * 8 : 64 + (e + 1) * 8, :] = gfull[e, 2]
    for part in range(2):
        finish_all(phase1(part), SPACE)
        finish_all(phase2(part), SPACE)
    finish_all(scatter, EVENTS)
    finish_all(gather, EVENTS)
    for i in range(4):
        halo_up(i).wait_send()
        halo_down(i).wait_send()


def shards(
    adjoint_start,
    checkpoints,
    sound_speed,
    wind_field,
    neighbours,
    halo_faces,
    send_list,
    recv_slots,
    event_source,
    source_wave,
):
    del neighbours
    vmem = pl.BlockSpec(memory_space=pltpu.VMEM)
    anywhere = pl.BlockSpec(memory_space=pl.ANY)
    nodes = (4, 4, 4, 8, 128)
    dma = pltpu.SemaphoreType.DMA
    end, speed, wind = pl.pallas_call(
        kernel,
        out_shape=(
            jax.ShapeDtypeStruct((ELEMS, ELEMS), F32),
            jax.ShapeDtypeStruct((64, ELEMS), F32),
            jax.ShapeDtypeStruct((128, ELEMS), F32),
        ),
        in_specs=[anywhere] * 9,
        out_specs=(vmem, vmem, vmem),
        scratch_shapes=[
            pltpu.VMEM((ELEMS, ELEMS), F32),
            pltpu.VMEM((1024, ELEMS), BF16),
            pltpu.VMEM((64, ELEMS), F32),
            pltpu.VMEM((128, ELEMS), F32),
            pltpu.VMEM((2, 128), I32),
            pltpu.VMEM((SPACE, SPACE), I32),
            pltpu.VMEM((SPACE, SPACE), I32),
            pltpu.SMEM((1,), I32),
            pltpu.SMEM((1, 64), F32),
            pltpu.VMEM((4,) + nodes, F32),
            pltpu.VMEM(nodes, F32),
            pltpu.VMEM(nodes, F32),
            pltpu.VMEM(nodes, F32),
            pltpu.VMEM(nodes, F32),
            pltpu.VMEM(nodes, F32),
            pltpu.VMEM(nodes, F32),
            pltpu.VMEM(nodes, F32),
            pltpu.VMEM(nodes, F32),
            pltpu.VMEM((2, 4, 4, 8, 128), F32),
            pltpu.VMEM((2, 4, 4, 8, 128), F32),
            pltpu.VMEM((2, 4, 4, 8, 128), F32),
            pltpu.VMEM((64, 8, 128), F32),
            pltpu.VMEM((ELEMS, ELEMS), BF16),
            pltpu.VMEM((512, ELEMS), BF16),
            pltpu.VMEM((512, 512), BF16),
            pltpu.VMEM((2, ELEMS, 512), BF16),
            pltpu.VMEM((4, 2, 4, 16, 128), BF16),
            pltpu.VMEM((4, 2, 4, 16, 128), BF16),
            pltpu.VMEM((2, SPACE, 16, 256), BF16),
            pltpu.VMEM((2, SPACE, 16, 256), BF16),
            pltpu.VMEM((2, SPACE, 16, 256), BF16),
            pltpu.VMEM((2, SPACE, 16, 256), BF16),
            pltpu.VMEM((2,) + nodes, F32),
            pltpu.VMEM((3, 64, 8, 128), F32),
            pltpu.VMEM((EVENTS, 3, 2, 8, 128), F32),
            pltpu.VMEM((EVENTS, 3, 2, 8, 128), F32),
            pltpu.VMEM((EVENTS, 3, 8, ELEMS), F32),
            dma((9,)),
            dma((4, 2)),
            dma((4, 2)),
            dma((2, SPACE)),
            dma((2, SPACE)),
            dma((2, SPACE)),
            dma((2, SPACE)),
            dma((EVENTS,)),
            dma((EVENTS,)),
            dma((EVENTS,)),
            dma((EVENTS,)),
        ],
        compiler_params=pltpu.CompilerParams(
            collective_id=0, has_side_effects=True
        ),
        name="adjoint_step",
    )(
        adjoint_start.reshape(ELEMS, ELEMS),
        checkpoints.reshape(1024, ELEMS),
        sound_speed,
        wind_field.reshape(128, ELEMS),
        halo_faces,
        send_list,
        recv_slots,
        event_source,
        source_wave,
    )
    return (
        end.reshape(1, 4, 64, ELEMS),
        speed,
        wind.reshape(2, 64, ELEMS),
    )


def solution(mesh):
    return jax.shard_map(
        shards,
        mesh=mesh,
        in_specs=(
            P("event", None, None, "space"),
            P("event", None, None, None, "space"),
            P(None, "space"),
            P(None, None, "space"),
            P(None, "space"),
            P(None, "space"),
            P("space", None),
            P("space", None),
            P("event"),
            P("event", None),
        ),
        out_specs=(P("event", None, None, "space"), P(None, "space"), P(None, None, "space")),
        check_vma=False,
    )
```

```python
import functools
import math

import jax
import jax.numpy as jnp
import numpy as np
from jax import lax
from jax.experimental import pallas as pl
from jax.experimental.pallas import tpu as pltpu
from jax.sharding import PartitionSpec as P

MESH = pl.DeviceIdType.MESH
F32 = jnp.float32
BF16 = jnp.bfloat16
I32 = jnp.int32
TIME_STEP = 0.08
ELEMS = 256
SPACE = 32
EVENTS = 8


def derivative_matrix():
    inner_point = 1.0 / math.sqrt(5.0)
    points = np.array([-1.0, -inner_point, inner_point, 1.0])
    products = np.array(
        [np.prod([points[i] - points[k] for k in range(4) if k != i]) for i in range(4)]
    )
    derivative = np.zeros((4, 4))
    for i in range(4):
        for j in range(4):
            if i != j:
                derivative[i, j] = products[i] / (products[j] * (points[i] - points[j]))
            else:
                derivative[i, i] = sum((1.0 / (points[i] - points[k]) for k in range(4) if k != i))
    return derivative


TABLE = [[float(np.float32(v)) for v in row] for row in derivative_matrix()]
TABLE_LOW = [
    [float(np.float32(jnp.bfloat16(np.float32(v)))) for v in row] for row in derivative_matrix()
]


def iota(shape, dim):
    return lax.broadcasted_iota(I32, shape, dim)


def nn(a, b):
    return lax.dot_general(a, b, (((1,), (0,)), ((), ())), preferred_element_type=F32)


def nt(a, b):
    return lax.dot_general(a, b, (((1,), (1,)), ((), ())), preferred_element_type=F32)


def onehot(condition):
    return jnp.where(condition, 1.0, 0.0).astype(BF16)


def split3(x):
    high = x.astype(BF16)
    rest = x - high.astype(F32)
    middle = rest.astype(BF16)
    low = (rest - middle.astype(F32)).astype(BF16)
    return high, middle, low


def roll(x, shift, axis):
    return pltpu.roll(x, shift % x.shape[axis], axis)


def line(coefficients, pick):
    total = None
    for k in range(4):
        term = coefficients[k] * pick(k)
        total = term if total is None else total + term
    return total


def kernel(
    y_hbm,
    q_hbm,
    c_hbm,
    w_hbm,
    hf_hbm,
    sl_hbm,
    rs_hbm,
    es_hbm,
    wave_hbm,
    out_y,
    out_g,
    y_in,
    q_in,
    c_in,
    w_in,
    hf_in,
    sl_in,
    rs_in,
    es_in,
    wave_in,
    states,
    total,
    ge,
    gn,
    gu,
    tend,
    cc,
    w1,
    w2,
    pe,
    pn,
    pu,
    src,
    can,
    spread,
    onward,
    settle,
    halo_send,
    halo_recv,
    sbuf,
    rbuf,
    sbuf2,
    rbuf2,
    qa,
    acc,
    gsend,
    grecv,
    gown,
    end,
    in_sem,
    halo_ssem,
    halo_rsem,
    p1_ssem,
    p1_rsem,
    p2_ssem,
    p2_rsem,
    rs_ssem,
    rs_rsem,
    ag_ssem,
    ag_rsem,
    out_sem,
):
    me = lax.axis_index("space")
    ev = lax.axis_index("event")
    upper = lax.rem(me + 1, SPACE)
    lower = lax.rem(me + SPACE - 1, SPACE)

    inputs = (
        (sl_hbm, sl_in),
        (q_hbm, q_in),
        (hf_hbm, hf_in),
        (y_hbm, y_in),
        (c_hbm, c_in),
        (w_hbm, w_in),
        (rs_hbm, rs_in),
        (es_hbm, es_in),
        (wave_hbm, wave_in),
    )
    fetches = [
        pltpu.make_async_copy(source, target, in_sem.at[k])
        for k, (source, target) in enumerate(inputs)
    ]
    for fetch in fetches:
        fetch.start()

    barrier = pltpu.get_barrier_semaphore()

    def greet_space(d, carry):
        pl.semaphore_signal(
            barrier, inc=1, device_id={"space": lax.rem(me + d, SPACE)}, device_id_type=MESH
        )
        return carry

    def greet_event(d, carry):
        pl.semaphore_signal(
            barrier, inc=1, device_id={"event": lax.rem(ev + d, EVENTS)}, device_id_type=MESH
        )
        return carry

    lax.fori_loop(1, SPACE, greet_space, 0)
    lax.fori_loop(1, EVENTS, greet_event, 0)

    fetches[0].wait()
    wanted = sl_in[...]
    valid = jnp.where(wanted < ELEMS, 1.0, 0.0)
    n_col = jnp.sum(valid, axis=1, keepdims=True)
    n_row = nt(jnp.ones((8, SPACE), BF16), valid.astype(BF16))[0:1]
    offset_rows = jnp.bitwise_and(iota((SPACE, SPACE), 0) + SPACE - me, SPACE - 1)
    offset_cols = jnp.bitwise_and(iota((SPACE, SPACE), 1) + SPACE - me, SPACE - 1)
    back_rows = jnp.bitwise_and(me + SPACE - iota((SPACE, SPACE), 0), SPACE - 1)
    start_col = jnp.sum(jnp.where(offset_cols < offset_rows, n_row, 0.0), axis=1, keepdims=True)
    start_back = jnp.sum(jnp.where(offset_cols < back_rows, n_row, 0.0), axis=1, keepdims=True)
    end_row = jnp.sum(jnp.where(offset_rows <= offset_cols, n_col, 0.0), axis=0, keepdims=True)

    columns = iota((SPACE, ELEMS), 1)
    found = jnp.zeros((SPACE, ELEMS), F32)
    for r in range(SPACE):
        found = found + jnp.where(wanted[:, r : r + 1] == columns, start_col + float(r), 0.0)
    label = jnp.sum(found, axis=0, keepdims=True).astype(I32)
    spot = jnp.bitwise_and(label, 31) * 8 + lax.shift_right_logical(label, 5)
    pick = onehot(iota((ELEMS, ELEMS), 0) == spot)
    fetches[1].wait()

    def fill(part):
        pieces = [
            nt(pick, q_in[h * 512 + part * 256 : h * 512 + part * 256 + 256, :])
            for h in range(2)
        ]
        pieces = [piece.reshape(SPACE, 8, 256) for piece in pieces]
        sbuf[part] = jnp.concatenate(pieces, axis=1).astype(BF16)
        rbuf[part, me] = sbuf[part, me]

    def phase1(part):
        def copy(d):
            peer = lax.rem(me + d, SPACE)
            return pltpu.make_async_remote_copy(
                src_ref=sbuf.at[part, peer],
                dst_ref=rbuf.at[part, me],
                send_sem=p1_ssem.at[part],
                recv_sem=p1_rsem.at[part],
                device_id={"space": peer},
                device_id_type=MESH,
            )

        return copy

    def phase2(part):
        def copy(d):
            peer = lax.rem(me + d, SPACE)
            return pltpu.make_async_remote_copy(
                src_ref=sbuf2.at[part, peer],
                dst_ref=rbuf2.at[part, me],
                send_sem=p2_ssem.at[part],
                recv_sem=p2_rsem.at[part],
                device_id={"space": peer},
                device_id_type=MESH,
            )

        return copy

    def start_all(copy, count):
        def body(d, carry):
            copy(d).start()
            return carry

        lax.fori_loop(1, count, body, 0)

    def whole(sender, receiver, send_sem, recv_sem, axis, peer):
        return pltpu.make_async_remote_copy(
            src_ref=sender,
            dst_ref=receiver,
            send_sem=send_sem,
            recv_sem=recv_sem,
            device_id={axis: peer},
            device_id_type=MESH,
        )

    def whole1(part):
        rest = pl.ds(0, SPACE - 1)
        return whole(
            sbuf.at[part, rest], rbuf.at[part, rest], p1_ssem.at[part], p1_rsem.at[part], "space", upper
        )

    def whole2(part):
        rest = pl.ds(0, SPACE - 1)
        return whole(
            sbuf2.at[part, rest], rbuf2.at[part, rest], p2_ssem.at[part], p2_rsem.at[part], "space", upper
        )

    fill(0)
    pl.semaphore_wait(barrier, SPACE - 1 + EVENTS - 1)
    start_all(phase1(0), SPACE)
    fill(1)

    for fetch in fetches[2:]:
        fetch.wait()
    hf = hf_in[...]
    hf_row = jnp.concatenate([hf[0:1], hf[1:2]], axis=1)
    can[...] = onehot(iota((ELEMS, ELEMS), 0) == hf_row)
    even = jnp.bitwise_and(iota((1, 8, 128), 1), 1) == 0
    field = lax.shift_right_logical(iota((1, 8, 128), 1), 1)
    height = jnp.bitwise_and(iota((1, 8, 128), 2), 15)

    wide = iota((512, ELEMS), 0)
    spread[...] = onehot(
        iota((512, ELEMS), 1)
        == jnp.bitwise_and(lax.shift_right_logical(wide, 1), 3) * 64
        + lax.shift_right_logical(wide, 3)
    )
    spread_one = onehot(iota((512, 64), 1) == lax.shift_right_logical(iota((512, 64), 0), 3))

    def by_layer(rows):
        return jnp.where(
            even, rows[:, 0:128].reshape(64, 8, 128), rows[:, 128:256].reshape(64, 8, 128)
        )

    def to_slab(x, spreading):
        result = None
        for part in split3(x):
            moved = nn(spreading, nn(part, can[...]).astype(BF16))
            result = moved if result is None else result + moved
        return by_layer(result).reshape(4, 4, 4, 8, 128)

    states[0] = to_slab(y_in[...], spread[...])
    cc[...] = to_slab(c_in[...], spread_one)
    w1[...] = to_slab(w_in[0:64, :], spread_one)
    w2[...] = to_slab(w_in[64:128, :], spread_one)
    for side, (position, sign) in enumerate(((0, 1.0), (3, -1.0))):
        speed = cc[position]
        wind = sign * w1[position]
        pe[side] = 3.0 * (wind - (speed + jnp.abs(wind)))
        speed = cc[:, position]
        wind = sign * w2[:, position]
        pn[side] = 3.0 * (wind - (speed + jnp.abs(wind)))
        pu[side] = -3.0 * cc[:, :, position]
    cc[...] = jnp.where(field == 0, cc[...] * cc[...], 1.0)
    target = es_in[0] - me * ELEMS
    at_source = (jnp.concatenate([hf, hf, hf, hf], axis=0) == target).reshape(1, 8, 128)
    at_source = jnp.logical_and(at_source, field == 0)[0]

    def place_source(n, carry):
        src[n] = jnp.where(at_source, wave_in[0, n], 0.0)
        return carry

    lax.fori_loop(0, 64, place_source, 0)

    def halo_up(i):
        return pltpu.make_async_remote_copy(
            src_ref=halo_send.at[i, 1],
            dst_ref=halo_recv.at[i, 0],
            send_sem=halo_ssem.at[i, 1],
            recv_sem=halo_rsem.at[i, 0],
            device_id={"space": upper},
            device_id_type=MESH,
        )

    def halo_down(i):
        return pltpu.make_async_remote_copy(
            src_ref=halo_send.at[i, 0],
            dst_ref=halo_recv.at[i, 1],
            send_sem=halo_ssem.at[i, 0],
            recv_sem=halo_rsem.at[i, 1],
            device_id={"space": lower},
            device_id_type=MESH,
        )

    def send_halo(i):
        first = states[i, 0].reshape(16, 8, 128)
        last = states[i, 3].reshape(16, 8, 128)
        halo_send[i, 1] = (
            jnp.where(even, roll(last[8:16], 7, 1), last[0:8]).reshape(4, 16, 128).astype(BF16)
        )
        halo_send[i, 0] = (
            jnp.where(even, first[0:8], roll(first[8:16], 1, 1)).reshape(4, 16, 128).astype(BF16)
        )
        halo_up(i).start()
        halo_down(i).start()

    def section(i):
        y = states.at[i]
        first = y[0].reshape(16, 8, 128)
        last = y[3].reshape(16, 8, 128)
        for k in range(4):
            ge[k] = line(TABLE[k], lambda j: y[j])
            gn[:, k] = line(TABLE[k], lambda j: y[:, j])
            gu[:, :, k] = line(TABLE[k], lambda j: y[:, :, j])
        tend[...] = w1[...] * ge[...] + w2[...] * gn[...] + src[...].reshape(4, 4, 4, 8, 128)
        for side, (here, there, shift, sign) in enumerate(((0, 3, 16, 3.0), (3, 0, 112, -3.0))):
            outside = roll(y[:, there].reshape(16, 8, 128), shift, 2).reshape(4, 4, 8, 128)
            jump = y[:, here] - outside
            tend[:, here] += pn[side] * jump
            gn[:, here] += sign * jump
        for side, (here, there, shift, sign, wall) in enumerate(
            ((0, 3, 1, 3.0, 0), (3, 0, 127, -3.0, 15))
        ):
            outside = roll(y[:, :, there].reshape(16, 8, 128), shift, 2)
            outside = jnp.where(height == wall, 0.0, outside).reshape(4, 4, 8, 128)
            jump = y[:, :, here] - outside
            tend[:, :, here] += pu[side] * jump
            gu[:, :, here] += sign * jump
        halo_up(i).wait_recv()
        halo_down(i).wait_recv()
        arrived = halo_recv[i, 0].astype(F32).reshape(8, 8, 128)
        arrived = jnp.concatenate([roll(arrived, 7, 1), arrived], axis=0)
        outside = jnp.where(even, arrived, roll(last, 1, 1)).reshape(4, 4, 8, 128)
        jump = y[0] - outside
        tend[0] += pe[0] * jump
        ge[0] += 3.0 * jump
        arrived = halo_recv[i, 1].astype(F32).reshape(8, 8, 128)
        arrived = jnp.concatenate([roll(arrived, 1, 1), arrived], axis=0)
        outside = jnp.where(even, roll(first, 7, 1), arrived).reshape(4, 4, 8, 128)
        jump = y[3] - outside
        tend[3] += pe[1] * jump
        ge[3] += -3.0 * jump
        for a in range(4):
            east = ge[a].reshape(16, 8, 128)
            north = gn[a].reshape(16, 8, 128)
            up = gu[a].reshape(16, 8, 128)
            swapped = (
                roll(jnp.where(field == 0, east, jnp.where(field == 3, up, 0.0)), 2, 1)
                + roll(jnp.where(field == 1, east, jnp.where(field == 0, up, 0.0)), 6, 1)
                + roll(jnp.where(jnp.bitwise_and(field, 1) == 0, north, 0.0), 4, 1)
            )
            slope = tend[a] - cc[a] * swapped.reshape(4, 4, 8, 128)
            if i == 0:
                total[a] = slope
            elif i < 3:
                total[a] += 2.0 * slope
            else:
                total[a] = states[0, a] + (TIME_STEP / 6.0) * (total[a] + slope)
            if i < 3:
                states[i + 1, a] = states[0, a] + (TIME_STEP if i == 2 else TIME_STEP / 2) * slope

    k8 = iota((8, SPACE), 0) * 32 + me
    off8 = jnp.sum(jnp.where(end_row.astype(I32) <= k8, 1.0, 0.0), axis=1, keepdims=True)
    off = jnp.broadcast_to(off8.astype(I32).reshape(1, 8, 1), (64, 8, 1)).reshape(512, 1)
    row = iota((512, 1), 0)
    origin = (
        jnp.bitwise_and(lax.shift_right_logical(row, 4) - off + SPACE, SPACE - 1) * 16
        + jnp.bitwise_and(row, 15)
    )

    def relay(part):
        whole1(part).wait_recv()
        rows = nn(onward[...], rbuf[part].reshape(512, 256)).astype(BF16)
        sbuf2[part] = rows.reshape(SPACE, 16, 256)
        rbuf2[part, me] = sbuf2[part, me]
        start_all(phase2(part), SPACE)

    send_halo(0)
    start_all(phase1(1), SPACE)
    onward[...] = onehot(iota((512, 512), 1) == origin)
    section(0)
    send_halo(1)
    relay(0)
    section(1)
    send_halo(2)
    relay(1)
    section(2)
    send_halo(3)

    def rows_from_slab(parts, selectors):
        result = None
        for part in parts:
            pieces = [nn(selector, part).astype(BF16) for selector in selectors]
            moved = nt(jnp.concatenate(pieces, axis=1), can[...])
            result = moved if result is None else result + moved
        return result

    shape = (ELEMS, 512)
    wanted_row = (
        jnp.bitwise_and(iota(shape, 0), 63) * 8 + lax.shift_right_logical(iota(shape, 0), 6) * 2
    )
    gather_rows = [onehot(iota(shape, 1) == wanted_row + layer) for layer in range(2)]
    landing = rs_in[...]
    places = iota((SPACE, 512), 1)
    landed = jnp.zeros((SPACE, 512), F32)
    for r in range(SPACE):
        label = start_back.astype(I32) + r
        place = jnp.bitwise_and(label, 31) * 16 + lax.shift_right_logical(label, 5)
        column = landing[:, r : r + 1]
        hit = jnp.logical_and(places == place, column < ELEMS)
        landed = landed + jnp.where(hit, column.astype(F32) + 1.0, 0.0)
    land_row = jnp.sum(landed, axis=0, keepdims=True) - 1.0
    land_row = jnp.broadcast_to(land_row, (8, 512))
    eye = onehot(iota((ELEMS, ELEMS), 0) == iota((ELEMS, ELEMS), 1))
    hf_col = nt(eye, jnp.broadcast_to(hf_row, (8, ELEMS)).astype(F32).astype(BF16))[:, 0:1]

    for h in range(2):
        place_row = (land_row if h == 0 else roll(land_row, 8, 1))[0:1]
        settle[h] = onehot(hf_col == place_row)

    weights = [TIME_STEP / 6.0, TIME_STEP / 3.0, TIME_STEP / 3.0, TIME_STEP / 6.0]
    for part in range(2):
        whole2(part).wait_recv()
        for h in range(2):
            settled = nn(settle[h], rbuf2[part].reshape(512, 256)).astype(BF16)
            qa[h] = by_layer(nt(spread[...], settled)).reshape(4, 4, 4, 8, 128)
        for a in range(4):
            east = north = speed = None
            for h in range(2):
                i = 2 * h + part
                q = qa.at[h]
                d_east = line(TABLE_LOW[a], lambda j: q[j]).reshape(16, 8, 128)
                d_north = jnp.stack(
                    [line(TABLE_LOW[k], lambda j: q[a, j]) for k in range(4)], axis=0
                ).reshape(16, 8, 128)
                d_up = jnp.stack(
                    [line(TABLE_LOW[k], lambda j: q[a, :, j]) for k in range(4)], axis=1
                ).reshape(16, 8, 128)
                y = weights[i] * states[i, a].reshape(16, 8, 128)
                own = jnp.where(field == 0, y, 0.0)
                own = own + roll(own, 4, 1)
                own = own + roll(own, 2, 1)
                product = own * jnp.where(
                    field == 1,
                    d_east,
                    jnp.where(field == 2, d_north, jnp.where(field == 3, d_up, 0.0)),
                )
                east = y * d_east if east is None else east + y * d_east
                north = y * d_north if north is None else north + y * d_north
                speed = product if speed is None else speed + product
            rows = slice(a * 16, (a + 1) * 16)
            if part == 0:
                acc[0, rows] = speed
                acc[1, rows] = east
                acc[2, rows] = north
            else:
                acc[0, rows] += speed
                acc[1, rows] += east
                acc[2, rows] += north
    for g in range(3):
        sums = acc[g] + roll(acc[g], 4, 1)
        sums = (sums + roll(sums, 2, 1)).reshape(16, 4, 8, 128)
        packed = jnp.where(
            field == 0,
            sums[:, 0],
            jnp.where(field == 1, sums[:, 1], jnp.where(field == 2, sums[:, 2], sums[:, 3])),
        )
        gsend[:, g] = (-packed).reshape(EVENTS, 2, 8, 128)

    def scatter(d):
        peer = lax.rem(ev + d, EVENTS)
        return pltpu.make_async_remote_copy(
            src_ref=gsend.at[peer],
            dst_ref=grecv.at[ev],
            send_sem=rs_ssem.at[0],
            recv_sem=rs_rsem.at[0],
            device_id={"event": peer},
            device_id_type=MESH,
        )

    def gather(d):
        peer = lax.rem(ev + d, EVENTS)
        return pltpu.make_async_remote_copy(
            src_ref=gown,
            dst_ref=out_g.at[ev],
            send_sem=ag_ssem.at[0],
            recv_sem=ag_rsem.at[0],
            device_id={"event": peer},
            device_id_type=MESH,
        )

    grecv[ev] = gsend[ev]
    start_all(scatter, EVENTS)
    rest = pl.ds(0, EVENTS - 1)
    next_event = lax.rem(ev + 1, EVENTS)
    scattered = whole(
        gsend.at[rest], grecv.at[rest], rs_ssem.at[0], rs_rsem.at[0], "event", next_event
    )
    gathered = whole(
        gsend.at[rest], out_g.at[rest], ag_ssem.at[0], ag_rsem.at[0], "event", next_event
    )
    section(3)
    end[...] = rows_from_slab(split3(total[...].reshape(512, 128)), gather_rows).reshape(
        4, 64, ELEMS
    )
    to_hbm = pltpu.make_async_copy(end, out_y, out_sem.at[0])
    to_hbm.start()
    for part in range(2):
        whole1(part).wait_send()
        whole2(part).wait_send()
    for i in range(4):
        halo_up(i).wait_send()
        halo_down(i).wait_send()
    shape = (24, 48)
    node = jnp.bitwise_and(iota(shape, 0), 7)
    position = (
        lax.shift_right_logical(iota(shape, 0), 3) * 16
        + lax.shift_right_logical(node, 2) * 8
        + jnp.bitwise_and(node, 3) * 2
    )
    gather_rows = [onehot(iota(shape, 1) == position + layer) for layer in range(2)]
    scattered.wait_recv()
    scattered.wait_send()
    summed = grecv[0]
    for e in range(1, EVENTS):
        summed = summed + grecv[e]
    rows = rows_from_slab(split3(summed.reshape(48, 128)), gather_rows)
    speed = c_in[pl.ds(pl.multiple_of(ev * 8, 8), 8), :]
    gown[...] = jnp.concatenate([2.0 * speed * rows[0:8], rows[8:24]], axis=0).reshape(3, 8, ELEMS)
    own = pltpu.make_async_copy(gown, out_g.at[ev], out_sem.at[1])
    own.start()
    start_all(gather, EVENTS)
    gathered.wait_recv()
    gathered.wait_send()
    own.wait()
    to_hbm.wait()


def deliver(y_hbm, g_hbm, out_y, out_s, out_w, y, g, sem):
    steps = [(y_hbm.at[f], y.at[f], out_y.at[f]) for f in range(4)]
    steps += [(g_hbm.at[:, 0], g.at[0], out_s)]
    steps += [(g_hbm.at[:, 1 + d], g.at[1 + d], out_w.at[d]) for d in range(2)]
    arrive = [pltpu.make_async_copy(a, b, sem.at[0, k]) for k, (a, b, _) in enumerate(steps)]
    leave = [pltpu.make_async_copy(b, c, sem.at[1, k]) for k, (_, b, c) in enumerate(steps)]
    for copy in arrive:
        copy.start()
    for first, second in zip(arrive, leave):
        first.wait()
        second.start()
    for copy in leave:
        copy.wait()


def shards(
    adjoint_start,
    checkpoints,
    sound_speed,
    wind_field,
    neighbours,
    halo_faces,
    send_list,
    recv_slots,
    event_source,
    source_wave,
):
    del neighbours
    anywhere = pl.BlockSpec(memory_space=pl.ANY)
    nodes = (4, 4, 4, 8, 128)
    dma = pltpu.SemaphoreType.DMA
    end, gradients = pl.pallas_call(
        kernel,
        out_shape=(
            jax.ShapeDtypeStruct((4, 64, ELEMS), F32),
            jax.ShapeDtypeStruct((EVENTS, 3, 8, ELEMS), F32),
        ),
        in_specs=[anywhere] * 9,
        out_specs=(anywhere, anywhere),
        scratch_shapes=[
            pltpu.VMEM((ELEMS, ELEMS), F32),
            pltpu.VMEM((1024, ELEMS), BF16),
            pltpu.VMEM((64, ELEMS), F32),
            pltpu.VMEM((128, ELEMS), F32),
            pltpu.VMEM((2, 128), I32),
            pltpu.VMEM((SPACE, SPACE), I32),
            pltpu.VMEM((SPACE, SPACE), I32),
            pltpu.SMEM((1,), I32),
            pltpu.SMEM((1, 64), F32),
            pltpu.VMEM((4,) + nodes, F32),
            pltpu.VMEM(nodes, F32),
            pltpu.VMEM(nodes, F32),
            pltpu.VMEM(nodes, F32),
            pltpu.VMEM(nodes, F32),
            pltpu.VMEM(nodes, F32),
            pltpu.VMEM(nodes, F32),
            pltpu.VMEM(nodes, F32),
            pltpu.VMEM(nodes, F32),
            pltpu.VMEM((2, 4, 4, 8, 128), F32),
            pltpu.VMEM((2, 4, 4, 8, 128), F32),
            pltpu.VMEM((2, 4, 4, 8, 128), F32),
            pltpu.VMEM((64, 8, 128), F32),
            pltpu.VMEM((ELEMS, ELEMS), BF16),
            pltpu.VMEM((512, ELEMS), BF16),
            pltpu.VMEM((512, 512), BF16),
            pltpu.VMEM((2, ELEMS, 512), BF16),
            pltpu.VMEM((4, 2, 4, 16, 128), BF16),
            pltpu.VMEM((4, 2, 4, 16, 128), BF16),
            pltpu.VMEM((2, SPACE, 16, 256), BF16),
            pltpu.VMEM((2, SPACE, 16, 256), BF16),
            pltpu.VMEM((2, SPACE, 16, 256), BF16),
            pltpu.VMEM((2, SPACE, 16, 256), BF16),
            pltpu.VMEM((2,) + nodes, F32),
            pltpu.VMEM((3, 64, 8, 128), F32),
            pltpu.VMEM((EVENTS, 3, 2, 8, 128), F32),
            pltpu.VMEM((EVENTS, 3, 2, 8, 128), F32),
            pltpu.VMEM((3, 8, ELEMS), F32),
            pltpu.VMEM((4, 64, ELEMS), F32),
            dma((9,)),
            dma((4, 2)),
            dma((4, 2)),
            dma((2,)),
            dma((2,)),
            dma((2,)),
            dma((2,)),
            dma((1,)),
            dma((1,)),
            dma((1,)),
            dma((1,)),
            dma((2,)),
        ],
        compiler_params=pltpu.CompilerParams(
            collective_id=0, has_side_effects=True
        ),
        name="adjoint_step",
    )(
        adjoint_start.reshape(ELEMS, ELEMS),
        checkpoints.reshape(1024, ELEMS),
        sound_speed,
        wind_field.reshape(128, ELEMS),
        halo_faces,
        send_list,
        recv_slots,
        event_source,
        source_wave,
    )
    end, speed, wind = pl.pallas_call(
        deliver,
        out_shape=(
            jax.ShapeDtypeStruct((4, 64, ELEMS), F32),
            jax.ShapeDtypeStruct((EVENTS, 8, ELEMS), F32),
            jax.ShapeDtypeStruct((2, EVENTS, 8, ELEMS), F32),
        ),
        in_specs=[anywhere] * 2,
        out_specs=(anywhere,) * 3,
        scratch_shapes=[
            pltpu.VMEM((4, 64, ELEMS), F32),
            pltpu.VMEM((3, EVENTS, 8, ELEMS), F32),
            dma((2, 7)),
        ],
        name="deliver",
    )(end, gradients)
    return (
        end.reshape(1, 4, 64, ELEMS),
        speed.reshape(64, ELEMS),
        wind.reshape(2, 64, ELEMS),
    )


def solution(mesh):
    return jax.shard_map(
        shards,
        mesh=mesh,
        in_specs=(
            P("event", None, None, "space"),
            P("event", None, None, None, "space"),
            P(None, "space"),
            P(None, None, "space"),
            P(None, "space"),
            P(None, "space"),
            P("space", None),
            P("space", None),
            P("event"),
            P("event", None),
        ),
        out_specs=(P("event", None, None, "space"), P(None, "space"), P(None, None, "space")),
        check_vma=False,
    )
```

```python
import functools
import math

import jax
import jax.numpy as jnp
import numpy as np
from jax import lax
from jax.experimental import pallas as pl
from jax.experimental.pallas import tpu as pltpu
from jax.sharding import PartitionSpec as P

MESH = pl.DeviceIdType.MESH
F32 = jnp.float32
BF16 = jnp.bfloat16
I32 = jnp.int32
TIME_STEP = 0.08
ELEMS = 256
SPACE = 32
EVENTS = 8


def derivative_matrix():
    inner_point = 1.0 / math.sqrt(5.0)
    points = np.array([-1.0, -inner_point, inner_point, 1.0])
    products = np.array(
        [np.prod([points[i] - points[k] for k in range(4) if k != i]) for i in range(4)]
    )
    derivative = np.zeros((4, 4))
    for i in range(4):
        for j in range(4):
            if i != j:
                derivative[i, j] = products[i] / (products[j] * (points[i] - points[j]))
            else:
                derivative[i, i] = sum((1.0 / (points[i] - points[k]) for k in range(4) if k != i))
    return derivative


TABLE = [[float(np.float32(v)) for v in row] for row in derivative_matrix()]
TABLE_LOW = [
    [float(np.float32(jnp.bfloat16(np.float32(v)))) for v in row] for row in derivative_matrix()
]


def iota(shape, dim):
    return lax.broadcasted_iota(I32, shape, dim)


def nn(a, b):
    return lax.dot_general(a, b, (((1,), (0,)), ((), ())), preferred_element_type=F32)


def nt(a, b):
    return lax.dot_general(a, b, (((1,), (1,)), ((), ())), preferred_element_type=F32)


def onehot(condition):
    return jnp.where(condition, 1.0, 0.0).astype(BF16)


def split3(x):
    high = x.astype(BF16)
    rest = x - high.astype(F32)
    middle = rest.astype(BF16)
    low = (rest - middle.astype(F32)).astype(BF16)
    return high, middle, low


def roll(x, shift, axis):
    return pltpu.roll(x, shift % x.shape[axis], axis)


def line(coefficients, pick):
    total = None
    for k in range(4):
        term = coefficients[k] * pick(k)
        total = term if total is None else total + term
    return total


def kernel(
    y_hbm,
    q_hbm,
    c_hbm,
    w_hbm,
    hf_hbm,
    sl_hbm,
    rs_hbm,
    es_hbm,
    wave_hbm,
    out_y,
    out_g,
    y_in,
    q_in,
    c_in,
    w_in,
    hf_in,
    sl_in,
    rs_in,
    es_in,
    wave_in,
    states,
    total,
    ge,
    gn,
    gu,
    tend,
    cc,
    w1,
    w2,
    pe,
    pn,
    pu,
    src,
    can,
    spread,
    onward,
    settle,
    halo_send,
    halo_recv,
    sbuf,
    rbuf,
    sbuf2,
    rbuf2,
    qa,
    acc,
    gsend,
    grecv,
    gown,
    end,
    in_sem,
    halo_ssem,
    halo_rsem,
    p1_ssem,
    p1_rsem,
    p2_ssem,
    p2_rsem,
    rs_ssem,
    rs_rsem,
    ag_ssem,
    ag_rsem,
    out_sem,
):
    me = lax.axis_index("space")
    ev = lax.axis_index("event")
    upper = lax.rem(me + 1, SPACE)
    lower = lax.rem(me + SPACE - 1, SPACE)

    inputs = (
        (sl_hbm, sl_in),
        (q_hbm, q_in),
        (hf_hbm, hf_in),
        (y_hbm, y_in),
        (c_hbm, c_in),
        (w_hbm, w_in),
        (rs_hbm, rs_in),
        (es_hbm, es_in),
        (wave_hbm, wave_in),
    )
    fetches = [
        pltpu.make_async_copy(source, target, in_sem.at[k])
        for k, (source, target) in enumerate(inputs)
    ]
    for fetch in fetches:
        fetch.start()

    barrier = pltpu.get_barrier_semaphore()

    def greet_space(d, carry):
        pl.semaphore_signal(
            barrier, inc=1, device_id={"space": lax.rem(me + d, SPACE)}, device_id_type=MESH
        )
        return carry

    def greet_event(d, carry):
        pl.semaphore_signal(
            barrier, inc=1, device_id={"event": lax.rem(ev + d, EVENTS)}, device_id_type=MESH
        )
        return carry

    lax.fori_loop(1, SPACE, greet_space, 0)
    lax.fori_loop(1, EVENTS, greet_event, 0)

    fetches[0].wait()
    wanted = sl_in[...]
    valid = jnp.where(wanted < ELEMS, 1.0, 0.0)
    n_col = jnp.sum(valid, axis=1, keepdims=True)
    n_row = nt(jnp.ones((8, SPACE), BF16), valid.astype(BF16))[0:1]
    offset_rows = jnp.bitwise_and(iota((SPACE, SPACE), 0) + SPACE - me, SPACE - 1)
    offset_cols = jnp.bitwise_and(iota((SPACE, SPACE), 1) + SPACE - me, SPACE - 1)
    back_rows = jnp.bitwise_and(me + SPACE - iota((SPACE, SPACE), 0), SPACE - 1)
    start_col = jnp.sum(jnp.where(offset_cols < offset_rows, n_row, 0.0), axis=1, keepdims=True)
    start_back = jnp.sum(jnp.where(offset_cols < back_rows, n_row, 0.0), axis=1, keepdims=True)
    end_row = jnp.sum(jnp.where(offset_rows <= offset_cols, n_col, 0.0), axis=0, keepdims=True)

    columns = iota((SPACE, ELEMS), 1)
    found = jnp.zeros((SPACE, ELEMS), F32)
    for r in range(SPACE):
        found = found + jnp.where(wanted[:, r : r + 1] == columns, start_col + float(r), 0.0)
    label = jnp.sum(found, axis=0, keepdims=True).astype(I32)
    spot = jnp.bitwise_and(label, 31) * 8 + lax.shift_right_logical(label, 5)
    pick = onehot(iota((ELEMS, ELEMS), 0) == spot)
    fetches[1].wait()

    def fill(part):
        pieces = [
            nt(pick, q_in[h * 512 + part * 256 : h * 512 + part * 256 + 256, :])
            for h in range(2)
        ]
        pieces = [piece.reshape(SPACE, 8, 256) for piece in pieces]
        sbuf[part] = jnp.concatenate(pieces, axis=1).astype(BF16)
        rbuf[part, me] = sbuf[part, me]

    def phase1(part):
        def copy(d):
            peer = lax.rem(me + d, SPACE)
            return pltpu.make_async_remote_copy(
                src_ref=sbuf.at[part, peer],
                dst_ref=rbuf.at[part, me],
                send_sem=p1_ssem.at[part],
                recv_sem=p1_rsem.at[part],
                device_id={"space": peer},
                device_id_type=MESH,
            )

        return copy

    def phase2(part):
        def copy(d):
            peer = lax.rem(me + d, SPACE)
            return pltpu.make_async_remote_copy(
                src_ref=sbuf2.at[part, peer],
                dst_ref=rbuf2.at[part, me],
                send_sem=p2_ssem.at[part],
                recv_sem=p2_rsem.at[part],
                device_id={"space": peer},
                device_id_type=MESH,
            )

        return copy

    def start_all(copy, count):
        def body(d, carry):
            copy(d).start()
            return carry

        lax.fori_loop(1, count, body, 0)

    def whole(sender, receiver, send_sem, recv_sem, axis, peer):
        return pltpu.make_async_remote_copy(
            src_ref=sender,
            dst_ref=receiver,
            send_sem=send_sem,
            recv_sem=recv_sem,
            device_id={axis: peer},
            device_id_type=MESH,
        )

    def whole1(part):
        rest = pl.ds(0, SPACE - 1)
        return whole(
            sbuf.at[part, rest], rbuf.at[part, rest], p1_ssem.at[part], p1_rsem.at[part], "space", upper
        )

    def whole2(part):
        rest = pl.ds(0, SPACE - 1)
        return whole(
            sbuf2.at[part, rest], rbuf2.at[part, rest], p2_ssem.at[part], p2_rsem.at[part], "space", upper
        )

    fill(0)
    pl.semaphore_wait(barrier, SPACE - 1 + EVENTS - 1)
    start_all(phase1(0), SPACE)
    fill(1)

    for fetch in fetches[2:]:
        fetch.wait()
    hf = hf_in[...]
    hf_row = jnp.concatenate([hf[0:1], hf[1:2]], axis=1)
    can[...] = onehot(iota((ELEMS, ELEMS), 0) == hf_row)
    even = jnp.bitwise_and(iota((1, 8, 128), 1), 1) == 0
    field = lax.shift_right_logical(iota((1, 8, 128), 1), 1)
    height = jnp.bitwise_and(iota((1, 8, 128), 2), 15)

    wide = iota((512, ELEMS), 0)
    spread[...] = onehot(
        iota((512, ELEMS), 1)
        == jnp.bitwise_and(lax.shift_right_logical(wide, 1), 3) * 64
        + lax.shift_right_logical(wide, 3)
    )
    spread_one = onehot(iota((512, 64), 1) == lax.shift_right_logical(iota((512, 64), 0), 3))

    def by_layer(rows):
        return jnp.where(
            even, rows[:, 0:128].reshape(64, 8, 128), rows[:, 128:256].reshape(64, 8, 128)
        )

    def to_slab(x, spreading):
        result = None
        for part in split3(x):
            moved = nn(spreading, nn(part, can[...]).astype(BF16))
            result = moved if result is None else result + moved
        return by_layer(result).reshape(4, 4, 4, 8, 128)

    states[0] = to_slab(y_in[...], spread[...])
    cc[...] = to_slab(c_in[...], spread_one)
    w1[...] = to_slab(w_in[0:64, :], spread_one)
    w2[...] = to_slab(w_in[64:128, :], spread_one)
    for side, (position, sign) in enumerate(((0, 1.0), (3, -1.0))):
        speed = cc[position]
        wind = sign * w1[position]
        pe[side] = 3.0 * (wind - (speed + jnp.abs(wind)))
        speed = cc[:, position]
        wind = sign * w2[:, position]
        pn[side] = 3.0 * (wind - (speed + jnp.abs(wind)))
        pu[side] = -3.0 * cc[:, :, position]
    cc[...] = jnp.where(field == 0, cc[...] * cc[...], 1.0)
    target = es_in[0] - me * ELEMS
    at_source = (jnp.concatenate([hf, hf, hf, hf], axis=0) == target).reshape(1, 8, 128)
    at_source = jnp.logical_and(at_source, field == 0)[0]

    def place_source(n, carry):
        src[n] = jnp.where(at_source, wave_in[0, n], 0.0)
        return carry

    lax.fori_loop(0, 64, place_source, 0)

    def halo_up(i):
        return pltpu.make_async_remote_copy(
            src_ref=halo_send.at[i, 1],
            dst_ref=halo_recv.at[i, 0],
            send_sem=halo_ssem.at[i, 1],
            recv_sem=halo_rsem.at[i, 0],
            device_id={"space": upper},
            device_id_type=MESH,
        )

    def halo_down(i):
        return pltpu.make_async_remote_copy(
            src_ref=halo_send.at[i, 0],
            dst_ref=halo_recv.at[i, 1],
            send_sem=halo_ssem.at[i, 0],
            recv_sem=halo_rsem.at[i, 1],
            device_id={"space": lower},
            device_id_type=MESH,
        )

    def send_halo(i):
        first = states[i, 0].reshape(16, 8, 128)
        last = states[i, 3].reshape(16, 8, 128)
        halo_send[i, 1] = (
            jnp.where(even, roll(last[8:16], 7, 1), last[0:8]).reshape(4, 16, 128).astype(BF16)
        )
        halo_send[i, 0] = (
            jnp.where(even, first[0:8], roll(first[8:16], 1, 1)).reshape(4, 16, 128).astype(BF16)
        )
        halo_up(i).start()
        halo_down(i).start()

    def section(i):
        y = states.at[i]
        first = y[0].reshape(16, 8, 128)
        last = y[3].reshape(16, 8, 128)
        for k in range(4):
            ge[k] = line(TABLE[k], lambda j: y[j])
            gn[:, k] = line(TABLE[k], lambda j: y[:, j])
            gu[:, :, k] = line(TABLE[k], lambda j: y[:, :, j])
        tend[...] = w1[...] * ge[...] + w2[...] * gn[...] + src[...].reshape(4, 4, 4, 8, 128)
        for side, (here, there, shift, sign) in enumerate(((0, 3, 16, 3.0), (3, 0, 112, -3.0))):
            outside = roll(y[:, there].reshape(16, 8, 128), shift, 2).reshape(4, 4, 8, 128)
            jump = y[:, here] - outside
            tend[:, here] += pn[side] * jump
            gn[:, here] += sign * jump
        for side, (here, there, shift, sign, wall) in enumerate(
            ((0, 3, 1, 3.0, 0), (3, 0, 127, -3.0, 15))
        ):
            outside = roll(y[:, :, there].reshape(16, 8, 128), shift, 2)
            outside = jnp.where(height == wall, 0.0, outside).reshape(4, 4, 8, 128)
            jump = y[:, :, here] - outside
            tend[:, :, here] += pu[side] * jump
            gu[:, :, here] += sign * jump
        halo_up(i).wait_recv()
        halo_down(i).wait_recv()
        arrived = halo_recv[i, 0].astype(F32).reshape(8, 8, 128)
        arrived = jnp.concatenate([roll(arrived, 7, 1), arrived], axis=0)
        outside = jnp.where(even, arrived, roll(last, 1, 1)).reshape(4, 4, 8, 128)
        jump = y[0] - outside
        tend[0] += pe[0] * jump
        ge[0] += 3.0 * jump
        arrived = halo_recv[i, 1].astype(F32).reshape(8, 8, 128)
        arrived = jnp.concatenate([roll(arrived, 1, 1), arrived], axis=0)
        outside = jnp.where(even, roll(first, 7, 1), arrived).reshape(4, 4, 8, 128)
        jump = y[3] - outside
        tend[3] += pe[1] * jump
        ge[3] += -3.0 * jump
        for a in range(4):
            east = ge[a].reshape(16, 8, 128)
            north = gn[a].reshape(16, 8, 128)
            up = gu[a].reshape(16, 8, 128)
            swapped = (
                roll(jnp.where(field == 0, east, jnp.where(field == 3, up, 0.0)), 2, 1)
                + roll(jnp.where(field == 1, east, jnp.where(field == 0, up, 0.0)), 6, 1)
                + roll(jnp.where(jnp.bitwise_and(field, 1) == 0, north, 0.0), 4, 1)
            )
            slope = tend[a] - cc[a] * swapped.reshape(4, 4, 8, 128)
            if i == 0:
                total[a] = slope
            elif i < 3:
                total[a] += 2.0 * slope
            else:
                total[a] = states[0, a] + (TIME_STEP / 6.0) * (total[a] + slope)
            if i < 3:
                states[i + 1, a] = states[0, a] + (TIME_STEP if i == 2 else TIME_STEP / 2) * slope

    k8 = iota((8, SPACE), 0) * 32 + me
    off8 = jnp.sum(jnp.where(end_row.astype(I32) <= k8, 1.0, 0.0), axis=1, keepdims=True)
    off = jnp.broadcast_to(off8.astype(I32).reshape(1, 8, 1), (64, 8, 1)).reshape(512, 1)
    row = iota((512, 1), 0)
    origin = (
        jnp.bitwise_and(lax.shift_right_logical(row, 4) - off + SPACE, SPACE - 1) * 16
        + jnp.bitwise_and(row, 15)
    )

    def relay(part):
        whole1(part).wait_recv()
        rows = nn(onward[...], rbuf[part].reshape(512, 256)).astype(BF16)
        sbuf2[part] = rows.reshape(SPACE, 16, 256)
        rbuf2[part, me] = sbuf2[part, me]
        start_all(phase2(part), SPACE)

    send_halo(0)
    start_all(phase1(1), SPACE)
    onward[...] = onehot(iota((512, 512), 1) == origin)
    section(0)
    send_halo(1)
    relay(0)
    section(1)
    send_halo(2)
    relay(1)
    section(2)
    send_halo(3)

    def rows_from_slab(parts, selectors):
        result = None
        for part in parts:
            pieces = [nn(selector, part).astype(BF16) for selector in selectors]
            moved = nt(jnp.concatenate(pieces, axis=1), can[...])
            result = moved if result is None else result + moved
        return result

    shape = (ELEMS, 512)
    wanted_row = (
        jnp.bitwise_and(iota(shape, 0), 63) * 8 + lax.shift_right_logical(iota(shape, 0), 6) * 2
    )
    gather_rows = [onehot(iota(shape, 1) == wanted_row + layer) for layer in range(2)]
    landing = rs_in[...]
    places = iota((SPACE, 512), 1)
    landed = jnp.zeros((SPACE, 512), F32)
    for r in range(SPACE):
        label = start_back.astype(I32) + r
        place = jnp.bitwise_and(label, 31) * 16 + lax.shift_right_logical(label, 5)
        column = landing[:, r : r + 1]
        hit = jnp.logical_and(places == place, column < ELEMS)
        landed = landed + jnp.where(hit, column.astype(F32) + 1.0, 0.0)
    land_row = jnp.sum(landed, axis=0, keepdims=True) - 1.0
    land_row = jnp.broadcast_to(land_row, (8, 512))
    eye = onehot(iota((ELEMS, ELEMS), 0) == iota((ELEMS, ELEMS), 1))
    hf_col = nt(eye, jnp.broadcast_to(hf_row, (8, ELEMS)).astype(F32).astype(BF16))[:, 0:1]

    for h in range(2):
        place_row = (land_row if h == 0 else roll(land_row, 8, 1))[0:1]
        settle[h] = onehot(hf_col == place_row)

    weights = [TIME_STEP / 6.0, TIME_STEP / 3.0, TIME_STEP / 3.0, TIME_STEP / 6.0]
    for part in range(2):
        whole2(part).wait_recv()
        for h in range(2):
            settled = nn(settle[h], rbuf2[part].reshape(512, 256)).astype(BF16)
            qa[h] = by_layer(nt(spread[...], settled)).reshape(4, 4, 4, 8, 128)
        for a in range(4):
            east = north = speed = None
            for h in range(2):
                i = 2 * h + part
                q = qa.at[h]
                d_east = line(TABLE_LOW[a], lambda j: q[j]).reshape(16, 8, 128)
                d_north = jnp.stack(
                    [line(TABLE_LOW[k], lambda j: q[a, j]) for k in range(4)], axis=0
                ).reshape(16, 8, 128)
                d_up = jnp.stack(
                    [line(TABLE_LOW[k], lambda j: q[a, :, j]) for k in range(4)], axis=1
                ).reshape(16, 8, 128)
                y = weights[i] * states[i, a].reshape(16, 8, 128)
                own = jnp.where(field == 0, y, 0.0)
                own = own + roll(own, 4, 1)
                own = own + roll(own, 2, 1)
                product = own * jnp.where(
                    field == 1,
                    d_east,
                    jnp.where(field == 2, d_north, jnp.where(field == 3, d_up, 0.0)),
                )
                east = y * d_east if east is None else east + y * d_east
                north = y * d_north if north is None else north + y * d_north
                speed = product if speed is None else speed + product
            rows = slice(a * 16, (a + 1) * 16)
            if part == 0:
                acc[0, rows] = speed
                acc[1, rows] = east
                acc[2, rows] = north
            else:
                acc[0, rows] += speed
                acc[1, rows] += east
                acc[2, rows] += north
    for g in range(3):
        sums = acc[g] + roll(acc[g], 4, 1)
        sums = (sums + roll(sums, 2, 1)).reshape(16, 4, 8, 128)
        packed = jnp.where(
            field == 0,
            sums[:, 0],
            jnp.where(field == 1, sums[:, 1], jnp.where(field == 2, sums[:, 2], sums[:, 3])),
        )
        gsend[:, g] = (-packed).reshape(EVENTS, 2, 8, 128)

    def scatter(d):
        peer = lax.rem(ev + d, EVENTS)
        return pltpu.make_async_remote_copy(
            src_ref=gsend.at[peer],
            dst_ref=grecv.at[ev],
            send_sem=rs_ssem.at[0],
            recv_sem=rs_rsem.at[0],
            device_id={"event": peer},
            device_id_type=MESH,
        )

    def gather(d):
        peer = lax.rem(ev + d, EVENTS)
        return pltpu.make_async_remote_copy(
            src_ref=gown,
            dst_ref=out_g.at[ev],
            send_sem=ag_ssem.at[0],
            recv_sem=ag_rsem.at[0],
            device_id={"event": peer},
            device_id_type=MESH,
        )

    grecv[ev] = gsend[ev]
    for d in (4, 5, 3, 2, 6, 7, 1):
        scatter(d).start()
    rest = pl.ds(0, EVENTS - 1)
    next_event = lax.rem(ev + 1, EVENTS)
    scattered = whole(
        gsend.at[rest], grecv.at[rest], rs_ssem.at[0], rs_rsem.at[0], "event", next_event
    )
    gathered = whole(
        gsend.at[rest], out_g.at[rest], ag_ssem.at[0], ag_rsem.at[0], "event", next_event
    )
    section(3)
    end[...] = rows_from_slab(split3(total[...].reshape(512, 128)), gather_rows).reshape(
        4, 64, ELEMS
    )
    to_hbm = pltpu.make_async_copy(end, out_y, out_sem.at[0])
    to_hbm.start()
    for part in range(2):
        whole1(part).wait_send()
        whole2(part).wait_send()
    for i in range(4):
        halo_up(i).wait_send()
        halo_down(i).wait_send()
    shape = (24, 48)
    node = jnp.bitwise_and(iota(shape, 0), 7)
    position = (
        lax.shift_right_logical(iota(shape, 0), 3) * 16
        + lax.shift_right_logical(node, 2) * 8
        + jnp.bitwise_and(node, 3) * 2
    )
    gather_rows = [onehot(iota(shape, 1) == position + layer) for layer in range(2)]
    scattered.wait_recv()
    summed = grecv[0]
    for e in range(1, EVENTS):
        summed = summed + grecv[e]
    rows = rows_from_slab(split3(summed.reshape(48, 128)), gather_rows)
    speed = c_in[pl.ds(pl.multiple_of(ev * 8, 8), 8), :]
    gown[...] = jnp.concatenate([2.0 * speed * rows[0:8], rows[8:24]], axis=0).reshape(3, 8, ELEMS)
    own = pltpu.make_async_copy(gown, out_g.at[ev], out_sem.at[1])
    own.start()
    for d in (4, 5, 3, 2, 6, 7, 1):
        gather(d).start()
    scattered.wait_send()
    gathered.wait_recv()
    gathered.wait_send()
    own.wait()
    to_hbm.wait()


def deliver(y_hbm, g_hbm, out_y, out_s, out_w, y, g, sem):
    steps = [(y_hbm.at[f], y.at[f], out_y.at[f]) for f in range(4)]
    steps += [(g_hbm.at[:, 0], g.at[0], out_s)]
    steps += [(g_hbm.at[:, 1 + d], g.at[1 + d], out_w.at[d]) for d in range(2)]
    arrive = [pltpu.make_async_copy(a, b, sem.at[0, k]) for k, (a, b, _) in enumerate(steps)]
    leave = [pltpu.make_async_copy(b, c, sem.at[1, k]) for k, (_, b, c) in enumerate(steps)]
    for copy in arrive:
        copy.start()
    for first, second in zip(arrive, leave):
        first.wait()
        second.start()
    for copy in leave:
        copy.wait()


def shards(
    adjoint_start,
    checkpoints,
    sound_speed,
    wind_field,
    neighbours,
    halo_faces,
    send_list,
    recv_slots,
    event_source,
    source_wave,
):
    del neighbours
    anywhere = pl.BlockSpec(memory_space=pl.ANY)
    nodes = (4, 4, 4, 8, 128)
    dma = pltpu.SemaphoreType.DMA
    end, gradients = pl.pallas_call(
        kernel,
        out_shape=(
            jax.ShapeDtypeStruct((4, 64, ELEMS), F32),
            jax.ShapeDtypeStruct((EVENTS, 3, 8, ELEMS), F32),
        ),
        in_specs=[anywhere] * 9,
        out_specs=(anywhere, anywhere),
        scratch_shapes=[
            pltpu.VMEM((ELEMS, ELEMS), F32),
            pltpu.VMEM((1024, ELEMS), BF16),
            pltpu.VMEM((64, ELEMS), F32),
            pltpu.VMEM((128, ELEMS), F32),
            pltpu.VMEM((2, 128), I32),
            pltpu.VMEM((SPACE, SPACE), I32),
            pltpu.VMEM((SPACE, SPACE), I32),
            pltpu.SMEM((1,), I32),
            pltpu.SMEM((1, 64), F32),
            pltpu.VMEM((4,) + nodes, F32),
            pltpu.VMEM(nodes, F32),
            pltpu.VMEM(nodes, F32),
            pltpu.VMEM(nodes, F32),
            pltpu.VMEM(nodes, F32),
            pltpu.VMEM(nodes, F32),
            pltpu.VMEM(nodes, F32),
            pltpu.VMEM(nodes, F32),
            pltpu.VMEM(nodes, F32),
            pltpu.VMEM((2, 4, 4, 8, 128), F32),
            pltpu.VMEM((2, 4, 4, 8, 128), F32),
            pltpu.VMEM((2, 4, 4, 8, 128), F32),
            pltpu.VMEM((64, 8, 128), F32),
            pltpu.VMEM((ELEMS, ELEMS), BF16),
            pltpu.VMEM((512, ELEMS), BF16),
            pltpu.VMEM((512, 512), BF16),
            pltpu.VMEM((2, ELEMS, 512), BF16),
            pltpu.VMEM((4, 2, 4, 16, 128), BF16),
            pltpu.VMEM((4, 2, 4, 16, 128), BF16),
            pltpu.VMEM((2, SPACE, 16, 256), BF16),
            pltpu.VMEM((2, SPACE, 16, 256), BF16),
            pltpu.VMEM((2, SPACE, 16, 256), BF16),
            pltpu.VMEM((2, SPACE, 16, 256), BF16),
            pltpu.VMEM((2,) + nodes, F32),
            pltpu.VMEM((3, 64, 8, 128), F32),
            pltpu.VMEM((EVENTS, 3, 2, 8, 128), F32),
            pltpu.VMEM((EVENTS, 3, 2, 8, 128), F32),
            pltpu.VMEM((3, 8, ELEMS), F32),
            pltpu.VMEM((4, 64, ELEMS), F32),
            dma((9,)),
            dma((4, 2)),
            dma((4, 2)),
            dma((2,)),
            dma((2,)),
            dma((2,)),
            dma((2,)),
            dma((1,)),
            dma((1,)),
            dma((1,)),
            dma((1,)),
            dma((2,)),
        ],
        compiler_params=pltpu.CompilerParams(
            collective_id=0, has_side_effects=True
        ),
        name="adjoint_step",
    )(
        adjoint_start.reshape(ELEMS, ELEMS),
        checkpoints.reshape(1024, ELEMS),
        sound_speed,
        wind_field.reshape(128, ELEMS),
        halo_faces,
        send_list,
        recv_slots,
        event_source,
        source_wave,
    )
    end, speed, wind = pl.pallas_call(
        deliver,
        out_shape=(
            jax.ShapeDtypeStruct((4, 64, ELEMS), F32),
            jax.ShapeDtypeStruct((EVENTS, 8, ELEMS), F32),
            jax.ShapeDtypeStruct((2, EVENTS, 8, ELEMS), F32),
        ),
        in_specs=[anywhere] * 2,
        out_specs=(anywhere,) * 3,
        scratch_shapes=[
            pltpu.VMEM((4, 64, ELEMS), F32),
            pltpu.VMEM((3, EVENTS, 8, ELEMS), F32),
            dma((2, 7)),
        ],
        name="deliver",
    )(end, gradients)
    return (
        end.reshape(1, 4, 64, ELEMS),
        speed.reshape(64, ELEMS),
        wind.reshape(2, 64, ELEMS),
    )


def solution(mesh):
    return jax.shard_map(
        shards,
        mesh=mesh,
        in_specs=(
            P("event", None, None, "space"),
            P("event", None, None, None, "space"),
            P(None, "space"),
            P(None, None, "space"),
            P(None, "space"),
            P(None, "space"),
            P("space", None),
            P("space", None),
            P("event"),
            P("event", None),
        ),
        out_specs=(P("event", None, None, "space"), P(None, "space"), P(None, None, "space")),
        check_vma=False,
    )
```

```python
import functools
import math

import jax
import jax.numpy as jnp
import numpy as np
from jax import lax
from jax.experimental import pallas as pl
from jax.experimental.pallas import tpu as pltpu
from jax.sharding import PartitionSpec as P

MESH = pl.DeviceIdType.MESH
F32 = jnp.float32
BF16 = jnp.bfloat16
I32 = jnp.int32
TIME_STEP = 0.08
ELEMS = 256
SPACE = 32
EVENTS = 8
FARTHEST_FIRST = sorted(
    range(1, SPACE), key=lambda d: -(min(d // 8, 4 - d // 8) + min(d % 8, 8 - d % 8))
)


def derivative_matrix():
    inner_point = 1.0 / math.sqrt(5.0)
    points = np.array([-1.0, -inner_point, inner_point, 1.0])
    products = np.array(
        [np.prod([points[i] - points[k] for k in range(4) if k != i]) for i in range(4)]
    )
    derivative = np.zeros((4, 4))
    for i in range(4):
        for j in range(4):
            if i != j:
                derivative[i, j] = products[i] / (products[j] * (points[i] - points[j]))
            else:
                derivative[i, i] = sum((1.0 / (points[i] - points[k]) for k in range(4) if k != i))
    return derivative


TABLE = [[float(np.float32(v)) for v in row] for row in derivative_matrix()]
TABLE_LOW = [
    [float(np.float32(jnp.bfloat16(np.float32(v)))) for v in row] for row in derivative_matrix()
]


def iota(shape, dim):
    return lax.broadcasted_iota(I32, shape, dim)


def nn(a, b):
    return lax.dot_general(a, b, (((1,), (0,)), ((), ())), preferred_element_type=F32)


def nt(a, b):
    return lax.dot_general(a, b, (((1,), (1,)), ((), ())), preferred_element_type=F32)


def onehot(condition):
    return jnp.where(condition, 1.0, 0.0).astype(BF16)


def split3(x):
    high = x.astype(BF16)
    rest = x - high.astype(F32)
    middle = rest.astype(BF16)
    low = (rest - middle.astype(F32)).astype(BF16)
    return high, middle, low


def roll(x, shift, axis):
    return pltpu.roll(x, shift % x.shape[axis], axis)


def line(coefficients, pick):
    total = None
    for k in range(4):
        term = coefficients[k] * pick(k)
        total = term if total is None else total + term
    return total


def kernel(
    y_hbm,
    q_hbm,
    c_hbm,
    w_hbm,
    hf_hbm,
    sl_hbm,
    rs_hbm,
    es_hbm,
    wave_hbm,
    out_y,
    out_g,
    y_in,
    q_in,
    c_in,
    w_in,
    hf_in,
    sl_in,
    rs_in,
    es_in,
    wave_in,
    states,
    total,
    ge,
    gn,
    gu,
    tend,
    cc,
    w1,
    w2,
    pe,
    pn,
    pu,
    src,
    can,
    spread,
    onward,
    settle,
    halo_send,
    halo_recv,
    sbuf,
    rbuf,
    sbuf2,
    rbuf2,
    qa,
    weighted,
    pressure,
    acc,
    gsend,
    grecv,
    gown,
    end,
    in_sem,
    halo_ssem,
    halo_rsem,
    p1_ssem,
    p1_rsem,
    p2_ssem,
    p2_rsem,
    rs_ssem,
    rs_rsem,
    ag_ssem,
    ag_rsem,
    out_sem,
):
    me = lax.axis_index("space")
    ev = lax.axis_index("event")
    upper = lax.rem(me + 1, SPACE)
    lower = lax.rem(me + SPACE - 1, SPACE)

    inputs = (
        (sl_hbm, sl_in),
        (q_hbm, q_in),
        (hf_hbm, hf_in),
        (y_hbm, y_in),
        (c_hbm, c_in),
        (w_hbm, w_in),
        (rs_hbm, rs_in),
        (es_hbm, es_in),
        (wave_hbm, wave_in),
    )
    fetches = [
        pltpu.make_async_copy(source, target, in_sem.at[k])
        for k, (source, target) in enumerate(inputs)
    ]
    for fetch in fetches:
        fetch.start()

    barrier = pltpu.get_barrier_semaphore()

    def greet_space(d, carry):
        pl.semaphore_signal(
            barrier, inc=1, device_id={"space": lax.rem(me + d, SPACE)}, device_id_type=MESH
        )
        return carry

    def greet_event(d, carry):
        pl.semaphore_signal(
            barrier, inc=1, device_id={"event": lax.rem(ev + d, EVENTS)}, device_id_type=MESH
        )
        return carry

    lax.fori_loop(1, SPACE, greet_space, 0)
    lax.fori_loop(1, EVENTS, greet_event, 0)

    fetches[0].wait()
    wanted = sl_in[...]
    valid = jnp.where(wanted < ELEMS, 1.0, 0.0)
    n_col = jnp.sum(valid, axis=1, keepdims=True)
    n_row = nt(jnp.ones((8, SPACE), BF16), valid.astype(BF16))[0:1]
    offset_rows = jnp.bitwise_and(iota((SPACE, SPACE), 0) + SPACE - me, SPACE - 1)
    offset_cols = jnp.bitwise_and(iota((SPACE, SPACE), 1) + SPACE - me, SPACE - 1)
    back_rows = jnp.bitwise_and(me + SPACE - iota((SPACE, SPACE), 0), SPACE - 1)
    start_col = jnp.sum(jnp.where(offset_cols < offset_rows, n_row, 0.0), axis=1, keepdims=True)
    start_back = jnp.sum(jnp.where(offset_cols < back_rows, n_row, 0.0), axis=1, keepdims=True)
    end_row = jnp.sum(jnp.where(offset_rows <= offset_cols, n_col, 0.0), axis=0, keepdims=True)

    columns = iota((SPACE, ELEMS), 1)
    found = jnp.zeros((SPACE, ELEMS), F32)
    for r in range(SPACE):
        found = found + jnp.where(wanted[:, r : r + 1] == columns, start_col + float(r), 0.0)
    label = jnp.sum(found, axis=0, keepdims=True).astype(I32)
    spot = jnp.bitwise_and(label, 31) * 8 + lax.shift_right_logical(label, 5)
    pick = onehot(iota((ELEMS, ELEMS), 0) == spot)
    fetches[1].wait()

    def fill(part):
        pieces = [
            nt(pick, q_in[h * 512 + part * 256 : h * 512 + part * 256 + 256, :])
            for h in range(2)
        ]
        pieces = [piece.reshape(SPACE, 8, 256) for piece in pieces]
        sbuf[part] = jnp.concatenate(pieces, axis=1).astype(BF16)
        rbuf[part, me] = sbuf[part, me]

    def phase1(part):
        def copy(d):
            peer = lax.rem(me + d, SPACE)
            return pltpu.make_async_remote_copy(
                src_ref=sbuf.at[part, peer],
                dst_ref=rbuf.at[part, me],
                send_sem=p1_ssem.at[part],
                recv_sem=p1_rsem.at[part],
                device_id={"space": peer},
                device_id_type=MESH,
            )

        return copy

    def phase2(part):
        def copy(d):
            peer = lax.rem(me + d, SPACE)
            return pltpu.make_async_remote_copy(
                src_ref=sbuf2.at[part, peer],
                dst_ref=rbuf2.at[part, me],
                send_sem=p2_ssem.at[part],
                recv_sem=p2_rsem.at[part],
                device_id={"space": peer},
                device_id_type=MESH,
            )

        return copy

    def start_all(copy):
        for d in FARTHEST_FIRST:
            copy(d).start()

    def whole(sender, receiver, send_sem, recv_sem, axis, peer):
        return pltpu.make_async_remote_copy(
            src_ref=sender,
            dst_ref=receiver,
            send_sem=send_sem,
            recv_sem=recv_sem,
            device_id={axis: peer},
            device_id_type=MESH,
        )

    def whole1(part):
        rest = pl.ds(0, SPACE - 1)
        return whole(
            sbuf.at[part, rest], rbuf.at[part, rest], p1_ssem.at[part], p1_rsem.at[part], "space", upper
        )

    def whole2(part):
        rest = pl.ds(0, SPACE - 1)
        return whole(
            sbuf2.at[part, rest], rbuf2.at[part, rest], p2_ssem.at[part], p2_rsem.at[part], "space", upper
        )

    fill(0)
    pl.semaphore_wait(barrier, SPACE - 1 + EVENTS - 1)
    start_all(phase1(0))

    for fetch in fetches[2:]:
        fetch.wait()
    hf = hf_in[...]
    hf_row = jnp.concatenate([hf[0:1], hf[1:2]], axis=1)
    can[...] = onehot(iota((ELEMS, ELEMS), 0) == hf_row)
    even = jnp.bitwise_and(iota((1, 8, 128), 1), 1) == 0
    field = lax.shift_right_logical(iota((1, 8, 128), 1), 1)
    height = jnp.bitwise_and(iota((1, 8, 128), 2), 15)

    wide = iota((512, ELEMS), 0)
    spread[...] = onehot(
        iota((512, ELEMS), 1)
        == jnp.bitwise_and(lax.shift_right_logical(wide, 1), 3) * 64
        + lax.shift_right_logical(wide, 3)
    )
    spread_one = onehot(iota((512, 64), 1) == lax.shift_right_logical(iota((512, 64), 0), 3))

    def by_layer(rows):
        return jnp.where(
            even, rows[:, 0:128].reshape(64, 8, 128), rows[:, 128:256].reshape(64, 8, 128)
        )

    def to_slab(x, spreading):
        result = None
        for part in split3(x):
            moved = nn(spreading, nn(part, can[...]).astype(BF16))
            result = moved if result is None else result + moved
        return by_layer(result).reshape(4, 4, 4, 8, 128)

    states[0] = to_slab(y_in[...], spread[...])
    cc[...] = to_slab(c_in[...], spread_one)
    w1[...] = to_slab(w_in[0:64, :], spread_one)
    w2[...] = to_slab(w_in[64:128, :], spread_one)
    for side, (position, sign) in enumerate(((0, 1.0), (3, -1.0))):
        speed = cc[position]
        wind = sign * w1[position]
        pe[side] = 3.0 * (wind - (speed + jnp.abs(wind)))
        speed = cc[:, position]
        wind = sign * w2[:, position]
        pn[side] = 3.0 * (wind - (speed + jnp.abs(wind)))
        pu[side] = -3.0 * cc[:, :, position]
    cc[...] = jnp.where(field == 0, cc[...] * cc[...], 1.0)
    target = es_in[0] - me * ELEMS
    at_source = (jnp.concatenate([hf, hf, hf, hf], axis=0) == target).reshape(1, 8, 128)
    at_source = jnp.logical_and(at_source, field == 0)[0]

    def place_source(n, carry):
        src[n] = jnp.where(at_source, wave_in[0, n], 0.0)
        return carry

    lax.fori_loop(0, 64, place_source, 0)

    def halo_up(i):
        return pltpu.make_async_remote_copy(
            src_ref=halo_send.at[i, 1],
            dst_ref=halo_recv.at[i, 0],
            send_sem=halo_ssem.at[i, 1],
            recv_sem=halo_rsem.at[i, 0],
            device_id={"space": upper},
            device_id_type=MESH,
        )

    def halo_down(i):
        return pltpu.make_async_remote_copy(
            src_ref=halo_send.at[i, 0],
            dst_ref=halo_recv.at[i, 1],
            send_sem=halo_ssem.at[i, 0],
            recv_sem=halo_rsem.at[i, 1],
            device_id={"space": lower},
            device_id_type=MESH,
        )

    def send_halo(i):
        first = states[i, 0].reshape(16, 8, 128)
        last = states[i, 3].reshape(16, 8, 128)
        halo_send[i, 1] = (
            jnp.where(even, roll(last[8:16], 7, 1), last[0:8]).reshape(4, 16, 128).astype(BF16)
        )
        halo_send[i, 0] = (
            jnp.where(even, first[0:8], roll(first[8:16], 1, 1)).reshape(4, 16, 128).astype(BF16)
        )
        halo_up(i).start()
        halo_down(i).start()

    def section(i):
        y = states.at[i]
        first = y[0].reshape(16, 8, 128)
        last = y[3].reshape(16, 8, 128)
        for k in range(4):
            ge[k] = line(TABLE[k], lambda j: y[j])
            gn[:, k] = line(TABLE[k], lambda j: y[:, j])
            gu[:, :, k] = line(TABLE[k], lambda j: y[:, :, j])
        tend[...] = w1[...] * ge[...] + w2[...] * gn[...] + src[...].reshape(4, 4, 4, 8, 128)
        for side, (here, there, shift, sign) in enumerate(((0, 3, 16, 3.0), (3, 0, 112, -3.0))):
            outside = roll(y[:, there].reshape(16, 8, 128), shift, 2).reshape(4, 4, 8, 128)
            jump = y[:, here] - outside
            tend[:, here] += pn[side] * jump
            gn[:, here] += sign * jump
        for side, (here, there, shift, sign, wall) in enumerate(
            ((0, 3, 1, 3.0, 0), (3, 0, 127, -3.0, 15))
        ):
            outside = roll(y[:, :, there].reshape(16, 8, 128), shift, 2)
            outside = jnp.where(height == wall, 0.0, outside).reshape(4, 4, 8, 128)
            jump = y[:, :, here] - outside
            tend[:, :, here] += pu[side] * jump
            gu[:, :, here] += sign * jump
        halo_up(i).wait_recv()
        halo_down(i).wait_recv()
        arrived = halo_recv[i, 0].astype(F32).reshape(8, 8, 128)
        arrived = jnp.concatenate([roll(arrived, 7, 1), arrived], axis=0)
        outside = jnp.where(even, arrived, roll(last, 1, 1)).reshape(4, 4, 8, 128)
        jump = y[0] - outside
        tend[0] += pe[0] * jump
        ge[0] += 3.0 * jump
        arrived = halo_recv[i, 1].astype(F32).reshape(8, 8, 128)
        arrived = jnp.concatenate([roll(arrived, 1, 1), arrived], axis=0)
        outside = jnp.where(even, roll(first, 7, 1), arrived).reshape(4, 4, 8, 128)
        jump = y[3] - outside
        tend[3] += pe[1] * jump
        ge[3] += -3.0 * jump
        for a in range(4):
            east = ge[a].reshape(16, 8, 128)
            north = gn[a].reshape(16, 8, 128)
            up = gu[a].reshape(16, 8, 128)
            swapped = (
                roll(jnp.where(field == 0, east, jnp.where(field == 3, up, 0.0)), 2, 1)
                + roll(jnp.where(field == 1, east, jnp.where(field == 0, up, 0.0)), 6, 1)
                + roll(jnp.where(jnp.bitwise_and(field, 1) == 0, north, 0.0), 4, 1)
            )
            slope = tend[a] - cc[a] * swapped.reshape(4, 4, 8, 128)
            if i == 0:
                total[a] = slope
            elif i < 3:
                total[a] += 2.0 * slope
            else:
                total[a] = states[0, a] + (TIME_STEP / 6.0) * (total[a] + slope)
            if i < 3:
                states[i + 1, a] = states[0, a] + (TIME_STEP if i == 2 else TIME_STEP / 2) * slope

    k8 = iota((8, SPACE), 0) * 32 + me
    off8 = jnp.sum(jnp.where(end_row.astype(I32) <= k8, 1.0, 0.0), axis=1, keepdims=True)
    off = jnp.broadcast_to(off8.astype(I32).reshape(1, 8, 1), (64, 8, 1)).reshape(512, 1)
    row = iota((512, 1), 0)
    origin = (
        jnp.bitwise_and(lax.shift_right_logical(row, 4) - off + SPACE, SPACE - 1) * 16
        + jnp.bitwise_and(row, 15)
    )

    def relay(part):
        whole1(part).wait_recv()
        rows = nn(onward[...], rbuf[part].reshape(512, 256)).astype(BF16)
        sbuf2[part] = rows.reshape(SPACE, 16, 256)
        rbuf2[part, me] = sbuf2[part, me]
        start_all(phase2(part))

    send_halo(0)
    fill(1)
    start_all(phase1(1))
    onward[...] = onehot(iota((512, 512), 1) == origin)
    section(0)
    send_halo(1)
    relay(0)
    section(1)
    send_halo(2)
    relay(1)
    section(2)
    send_halo(3)

    def rows_from_slab(parts, selectors):
        result = None
        for part in parts:
            pieces = [nn(selector, part).astype(BF16) for selector in selectors]
            moved = nt(jnp.concatenate(pieces, axis=1), can[...])
            result = moved if result is None else result + moved
        return result

    shape = (ELEMS, 512)
    wanted_row = (
        jnp.bitwise_and(iota(shape, 0), 63) * 8 + lax.shift_right_logical(iota(shape, 0), 6) * 2
    )
    gather_rows = [onehot(iota(shape, 1) == wanted_row + layer) for layer in range(2)]
    landing = rs_in[...]
    places = iota((SPACE, 512), 1)
    landed = jnp.zeros((SPACE, 512), F32)
    for r in range(SPACE):
        label = start_back.astype(I32) + r
        place = jnp.bitwise_and(label, 31) * 16 + lax.shift_right_logical(label, 5)
        column = landing[:, r : r + 1]
        hit = jnp.logical_and(places == place, column < ELEMS)
        landed = landed + jnp.where(hit, column.astype(F32) + 1.0, 0.0)
    land_row = jnp.sum(landed, axis=0, keepdims=True) - 1.0
    land_row = jnp.broadcast_to(land_row, (8, 512))
    eye = onehot(iota((ELEMS, ELEMS), 0) == iota((ELEMS, ELEMS), 1))
    hf_col = nt(eye, jnp.broadcast_to(hf_row, (8, ELEMS)).astype(F32).astype(BF16))[:, 0:1]

    for h in range(2):
        place_row = (land_row if h == 0 else roll(land_row, 8, 1))[0:1]
        settle[h] = onehot(hf_col == place_row)

    weights = [TIME_STEP / 6.0, TIME_STEP / 3.0, TIME_STEP / 3.0, TIME_STEP / 6.0]
    for part in range(2):
        for h in range(2):
            i = 2 * h + part
            y = weights[i] * states[i].reshape(64, 8, 128)
            own = jnp.where(field == 0, y, 0.0)
            own = own + roll(own, 4, 1)
            weighted[h] = y
            pressure[h] = own + roll(own, 2, 1)
        whole2(part).wait_recv()
        for h in range(2):
            settled = nn(settle[h], rbuf2[part].reshape(512, 256)).astype(BF16)
            qa[h] = by_layer(nt(spread[...], settled)).reshape(4, 4, 4, 8, 128)
        for a in range(4):
            east = north = speed = None
            for h in range(2):
                q = qa.at[h]
                d_east = line(TABLE_LOW[a], lambda j: q[j]).reshape(16, 8, 128)
                d_north = jnp.stack(
                    [line(TABLE_LOW[k], lambda j: q[a, j]) for k in range(4)], axis=0
                ).reshape(16, 8, 128)
                d_up = jnp.stack(
                    [line(TABLE_LOW[k], lambda j: q[a, :, j]) for k in range(4)], axis=1
                ).reshape(16, 8, 128)
                y = weighted[h, a * 16 : (a + 1) * 16]
                own = pressure[h, a * 16 : (a + 1) * 16]
                product = own * jnp.where(
                    field == 1,
                    d_east,
                    jnp.where(field == 2, d_north, jnp.where(field == 3, d_up, 0.0)),
                )
                east = y * d_east if east is None else east + y * d_east
                north = y * d_north if north is None else north + y * d_north
                speed = product if speed is None else speed + product
            rows = slice(a * 16, (a + 1) * 16)
            if part == 0:
                acc[0, rows] = speed
                acc[1, rows] = east
                acc[2, rows] = north
            else:
                acc[0, rows] += speed
                acc[1, rows] += east
                acc[2, rows] += north
    for g in range(3):
        sums = acc[g] + roll(acc[g], 4, 1)
        sums = (sums + roll(sums, 2, 1)).reshape(16, 4, 8, 128)
        packed = jnp.where(
            field == 0,
            sums[:, 0],
            jnp.where(field == 1, sums[:, 1], jnp.where(field == 2, sums[:, 2], sums[:, 3])),
        )
        gsend[:, g] = (-packed).reshape(EVENTS, 2, 8, 128)

    def scatter(d):
        peer = lax.rem(ev + d, EVENTS)
        return pltpu.make_async_remote_copy(
            src_ref=gsend.at[peer],
            dst_ref=grecv.at[ev],
            send_sem=rs_ssem.at[0],
            recv_sem=rs_rsem.at[0],
            device_id={"event": peer},
            device_id_type=MESH,
        )

    def gather(d):
        peer = lax.rem(ev + d, EVENTS)
        return pltpu.make_async_remote_copy(
            src_ref=gown,
            dst_ref=out_g.at[ev],
            send_sem=ag_ssem.at[0],
            recv_sem=ag_rsem.at[0],
            device_id={"event": peer},
            device_id_type=MESH,
        )

    grecv[ev] = gsend[ev]
    for d in (4, 5, 3, 2, 6, 7, 1):
        scatter(d).start()
    rest = pl.ds(0, EVENTS - 1)
    next_event = lax.rem(ev + 1, EVENTS)
    scattered = whole(
        gsend.at[rest], grecv.at[rest], rs_ssem.at[0], rs_rsem.at[0], "event", next_event
    )
    gathered = whole(
        gsend.at[rest], out_g.at[rest], ag_ssem.at[0], ag_rsem.at[0], "event", next_event
    )
    section(3)
    end[...] = rows_from_slab(split3(total[...].reshape(512, 128)), gather_rows).reshape(
        4, 64, ELEMS
    )
    to_hbm = pltpu.make_async_copy(end, out_y, out_sem.at[0])
    to_hbm.start()
    for part in range(2):
        whole1(part).wait_send()
        whole2(part).wait_send()
    for i in range(4):
        halo_up(i).wait_send()
        halo_down(i).wait_send()
    shape = (24, 48)
    node = jnp.bitwise_and(iota(shape, 0), 7)
    position = (
        lax.shift_right_logical(iota(shape, 0), 3) * 16
        + lax.shift_right_logical(node, 2) * 8
        + jnp.bitwise_and(node, 3) * 2
    )
    gather_rows = [onehot(iota(shape, 1) == position + layer) for layer in range(2)]
    scattered.wait_recv()
    summed = grecv[0]
    for e in range(1, EVENTS):
        summed = summed + grecv[e]
    rows = rows_from_slab(split3(summed.reshape(48, 128)), gather_rows)
    speed = c_in[pl.ds(pl.multiple_of(ev * 8, 8), 8), :]
    gown[...] = jnp.concatenate([2.0 * speed * rows[0:8], rows[8:24]], axis=0).reshape(3, 8, ELEMS)
    own = pltpu.make_async_copy(gown, out_g.at[ev], out_sem.at[1])
    own.start()
    for d in (4, 5, 3, 2, 6, 7, 1):
        gather(d).start()
    scattered.wait_send()
    gathered.wait_recv()
    gathered.wait_send()
    own.wait()
    to_hbm.wait()


def deliver(y_hbm, g_hbm, out_y, out_s, out_w, y, g, sem):
    steps = [(y_hbm.at[f], y.at[f], out_y.at[f]) for f in range(4)]
    steps += [(g_hbm.at[:, 0], g.at[0], out_s)]
    steps += [(g_hbm.at[:, 1 + d], g.at[1 + d], out_w.at[d]) for d in range(2)]
    arrive = [pltpu.make_async_copy(a, b, sem.at[0, k]) for k, (a, b, _) in enumerate(steps)]
    leave = [pltpu.make_async_copy(b, c, sem.at[1, k]) for k, (_, b, c) in enumerate(steps)]
    for copy in arrive:
        copy.start()
    for first, second in zip(arrive, leave):
        first.wait()
        second.start()
    for copy in leave:
        copy.wait()


def shards(
    adjoint_start,
    checkpoints,
    sound_speed,
    wind_field,
    neighbours,
    halo_faces,
    send_list,
    recv_slots,
    event_source,
    source_wave,
):
    del neighbours
    anywhere = pl.BlockSpec(memory_space=pl.ANY)
    nodes = (4, 4, 4, 8, 128)
    dma = pltpu.SemaphoreType.DMA
    end, gradients = pl.pallas_call(
        kernel,
        out_shape=(
            jax.ShapeDtypeStruct((4, 64, ELEMS), F32),
            jax.ShapeDtypeStruct((EVENTS, 3, 8, ELEMS), F32),
        ),
        in_specs=[anywhere] * 9,
        out_specs=(anywhere, anywhere),
        scratch_shapes=[
            pltpu.VMEM((ELEMS, ELEMS), F32),
            pltpu.VMEM((1024, ELEMS), BF16),
            pltpu.VMEM((64, ELEMS), F32),
            pltpu.VMEM((128, ELEMS), F32),
            pltpu.VMEM((2, 128), I32),
            pltpu.VMEM((SPACE, SPACE), I32),
            pltpu.VMEM((SPACE, SPACE), I32),
            pltpu.SMEM((1,), I32),
            pltpu.SMEM((1, 64), F32),
            pltpu.VMEM((4,) + nodes, F32),
            pltpu.VMEM(nodes, F32),
            pltpu.VMEM(nodes, F32),
            pltpu.VMEM(nodes, F32),
            pltpu.VMEM(nodes, F32),
            pltpu.VMEM(nodes, F32),
            pltpu.VMEM(nodes, F32),
            pltpu.VMEM(nodes, F32),
            pltpu.VMEM(nodes, F32),
            pltpu.VMEM((2, 4, 4, 8, 128), F32),
            pltpu.VMEM((2, 4, 4, 8, 128), F32),
            pltpu.VMEM((2, 4, 4, 8, 128), F32),
            pltpu.VMEM((64, 8, 128), F32),
            pltpu.VMEM((ELEMS, ELEMS), BF16),
            pltpu.VMEM((512, ELEMS), BF16),
            pltpu.VMEM((512, 512), BF16),
            pltpu.VMEM((2, ELEMS, 512), BF16),
            pltpu.VMEM((4, 2, 4, 16, 128), BF16),
            pltpu.VMEM((4, 2, 4, 16, 128), BF16),
            pltpu.VMEM((2, SPACE, 16, 256), BF16),
            pltpu.VMEM((2, SPACE, 16, 256), BF16),
            pltpu.VMEM((2, SPACE, 16, 256), BF16),
            pltpu.VMEM((2, SPACE, 16, 256), BF16),
            pltpu.VMEM((2,) + nodes, F32),
            pltpu.VMEM((2, 64, 8, 128), F32),
            pltpu.VMEM((2, 64, 8, 128), F32),
            pltpu.VMEM((3, 64, 8, 128), F32),
            pltpu.VMEM((EVENTS, 3, 2, 8, 128), F32),
            pltpu.VMEM((EVENTS, 3, 2, 8, 128), F32),
            pltpu.VMEM((3, 8, ELEMS), F32),
            pltpu.VMEM((4, 64, ELEMS), F32),
            dma((9,)),
            dma((4, 2)),
            dma((4, 2)),
            dma((2,)),
            dma((2,)),
            dma((2,)),
            dma((2,)),
            dma((1,)),
            dma((1,)),
            dma((1,)),
            dma((1,)),
            dma((2,)),
        ],
        compiler_params=pltpu.CompilerParams(
            collective_id=0, has_side_effects=True
        ),
        name="adjoint_step",
    )(
        adjoint_start.reshape(ELEMS, ELEMS),
        checkpoints.reshape(1024, ELEMS),
        sound_speed,
        wind_field.reshape(128, ELEMS),
        halo_faces,
        send_list,
        recv_slots,
        event_source,
        source_wave,
    )
    end, speed, wind = pl.pallas_call(
        deliver,
        out_shape=(
            jax.ShapeDtypeStruct((4, 64, ELEMS), F32),
            jax.ShapeDtypeStruct((EVENTS, 8, ELEMS), F32),
            jax.ShapeDtypeStruct((2, EVENTS, 8, ELEMS), F32),
        ),
        in_specs=[anywhere] * 2,
        out_specs=(anywhere,) * 3,
        scratch_shapes=[
            pltpu.VMEM((4, 64, ELEMS), F32),
            pltpu.VMEM((3, EVENTS, 8, ELEMS), F32),
            dma((2, 7)),
        ],
        name="deliver",
    )(end, gradients)
    return (
        end.reshape(1, 4, 64, ELEMS),
        speed.reshape(64, ELEMS),
        wind.reshape(2, 64, ELEMS),
    )


def solution(mesh):
    return jax.shard_map(
        shards,
        mesh=mesh,
        in_specs=(
            P("event", None, None, "space"),
            P("event", None, None, None, "space"),
            P(None, "space"),
            P(None, None, "space"),
            P(None, "space"),
            P(None, "space"),
            P("space", None),
            P("space", None),
            P("event"),
            P("event", None),
        ),
        out_specs=(P("event", None, None, "space"), P(None, "space"), P(None, None, "space")),
        check_vma=False,
    )
```

```python
import functools
import math

import jax
import jax.numpy as jnp
import numpy as np
from jax import lax
from jax.experimental import pallas as pl
from jax.experimental.pallas import tpu as pltpu
from jax.sharding import PartitionSpec as P

MESH = pl.DeviceIdType.MESH
F32 = jnp.float32
BF16 = jnp.bfloat16
I32 = jnp.int32
TIME_STEP = 0.08
ELEMS = 256
SPACE = 32
EVENTS = 8


def derivative_matrix():
    inner_point = 1.0 / math.sqrt(5.0)
    points = np.array([-1.0, -inner_point, inner_point, 1.0])
    products = np.array(
        [np.prod([points[i] - points[k] for k in range(4) if k != i]) for i in range(4)]
    )
    derivative = np.zeros((4, 4))
    for i in range(4):
        for j in range(4):
            if i != j:
                derivative[i, j] = products[i] / (products[j] * (points[i] - points[j]))
            else:
                derivative[i, i] = sum((1.0 / (points[i] - points[k]) for k in range(4) if k != i))
    return derivative


TABLE = [[float(np.float32(v)) for v in row] for row in derivative_matrix()]
TABLE_LOW = [
    [float(np.float32(jnp.bfloat16(np.float32(v)))) for v in row] for row in derivative_matrix()
]


def iota(shape, dim):
    return lax.broadcasted_iota(I32, shape, dim)


def nn(a, b):
    return lax.dot_general(a, b, (((1,), (0,)), ((), ())), preferred_element_type=F32)


def nt(a, b):
    return lax.dot_general(a, b, (((1,), (1,)), ((), ())), preferred_element_type=F32)


def onehot(condition):
    return jnp.where(condition, 1.0, 0.0).astype(BF16)


def split3(x):
    high = x.astype(BF16)
    rest = x - high.astype(F32)
    middle = rest.astype(BF16)
    low = (rest - middle.astype(F32)).astype(BF16)
    return high, middle, low


def roll(x, shift, axis):
    return pltpu.roll(x, shift % x.shape[axis], axis)


def line(coefficients, pick):
    total = None
    for k in range(4):
        term = coefficients[k] * pick(k)
        total = term if total is None else total + term
    return total


def kernel(
    y_hbm,
    q_hbm,
    c_hbm,
    w_hbm,
    hf_hbm,
    sl_hbm,
    rs_hbm,
    es_hbm,
    wave_hbm,
    out_y,
    out_g,
    y_in,
    q_in,
    c_in,
    w_in,
    hf_in,
    sl_in,
    rs_in,
    es_in,
    wave_in,
    states,
    total,
    ge,
    gn,
    gu,
    tend,
    cc,
    w1,
    w2,
    pe,
    pn,
    pu,
    src,
    can,
    spread,
    onward,
    settle,
    halo_send,
    halo_recv,
    sbuf,
    rbuf,
    sbuf2,
    rbuf2,
    qa,
    weighted,
    pressure,
    acc,
    gsend,
    grecv,
    gown,
    end,
    in_sem,
    halo_ssem,
    halo_rsem,
    p1_ssem,
    p1_rsem,
    p2_ssem,
    p2_rsem,
    rs_ssem,
    rs_rsem,
    ag_ssem,
    ag_rsem,
    out_sem,
):
    me = lax.axis_index("space")
    ev = lax.axis_index("event")
    upper = lax.rem(me + 1, SPACE)
    lower = lax.rem(me + SPACE - 1, SPACE)

    inputs = (
        (sl_hbm, sl_in),
        (q_hbm, q_in),
        (hf_hbm, hf_in),
        (y_hbm, y_in),
        (c_hbm, c_in),
        (w_hbm, w_in),
        (rs_hbm, rs_in),
        (es_hbm, es_in),
        (wave_hbm, wave_in),
    )
    fetches = [
        pltpu.make_async_copy(source, target, in_sem.at[k])
        for k, (source, target) in enumerate(inputs)
    ]
    for fetch in fetches:
        fetch.start()

    barrier = pltpu.get_barrier_semaphore()

    def greet_space(d, carry):
        pl.semaphore_signal(
            barrier, inc=1, device_id={"space": lax.rem(me + d, SPACE)}, device_id_type=MESH
        )
        return carry

    def greet_event(d, carry):
        pl.semaphore_signal(
            barrier, inc=1, device_id={"event": lax.rem(ev + d, EVENTS)}, device_id_type=MESH
        )
        return carry

    lax.fori_loop(1, SPACE, greet_space, 0)
    lax.fori_loop(1, EVENTS, greet_event, 0)

    fetches[0].wait()
    wanted = sl_in[...]
    valid = jnp.where(wanted < ELEMS, 1.0, 0.0)
    n_col = jnp.sum(valid, axis=1, keepdims=True)
    n_row = nt(jnp.ones((8, SPACE), BF16), valid.astype(BF16))[0:1]
    offset_rows = jnp.bitwise_and(iota((SPACE, SPACE), 0) + SPACE - me, SPACE - 1)
    offset_cols = jnp.bitwise_and(iota((SPACE, SPACE), 1) + SPACE - me, SPACE - 1)
    back_rows = jnp.bitwise_and(me + SPACE - iota((SPACE, SPACE), 0), SPACE - 1)
    start_col = jnp.sum(jnp.where(offset_cols < offset_rows, n_row, 0.0), axis=1, keepdims=True)
    start_back = jnp.sum(jnp.where(offset_cols < back_rows, n_row, 0.0), axis=1, keepdims=True)
    end_row = jnp.sum(jnp.where(offset_rows <= offset_cols, n_col, 0.0), axis=0, keepdims=True)

    columns = iota((SPACE, ELEMS), 1)
    found = jnp.zeros((SPACE, ELEMS), F32)
    for r in range(SPACE):
        found = found + jnp.where(wanted[:, r : r + 1] == columns, start_col + float(r), 0.0)
    label = jnp.sum(found, axis=0, keepdims=True).astype(I32)
    spot = jnp.bitwise_and(label, 31) * 8 + lax.shift_right_logical(label, 5)
    pick = onehot(iota((ELEMS, ELEMS), 0) == spot)
    fetches[1].wait()

    def fill(part):
        pieces = [
            nt(pick, q_in[h * 512 + part * 256 : h * 512 + part * 256 + 256, :])
            for h in range(2)
        ]
        pieces = [piece.reshape(SPACE, 8, 256) for piece in pieces]
        sbuf[part] = jnp.concatenate(pieces, axis=1).astype(BF16)
        rbuf[part, me] = sbuf[part, me]

    def phase1(part):
        def copy(d):
            peer = lax.rem(me + d, SPACE)
            return pltpu.make_async_remote_copy(
                src_ref=sbuf.at[part, peer],
                dst_ref=rbuf.at[part, me],
                send_sem=p1_ssem.at[part],
                recv_sem=p1_rsem.at[part],
                device_id={"space": peer},
                device_id_type=MESH,
            )

        return copy

    def phase2(part):
        def copy(d):
            peer = lax.rem(me + d, SPACE)
            return pltpu.make_async_remote_copy(
                src_ref=sbuf2.at[part, peer],
                dst_ref=rbuf2.at[part, me],
                send_sem=p2_ssem.at[part],
                recv_sem=p2_rsem.at[part],
                device_id={"space": peer},
                device_id_type=MESH,
            )

        return copy

    def start_all(copy):
        def body(d, carry):
            copy(d).start()
            return carry

        lax.fori_loop(1, SPACE, body, 0)

    def whole(sender, receiver, send_sem, recv_sem, axis, peer):
        return pltpu.make_async_remote_copy(
            src_ref=sender,
            dst_ref=receiver,
            send_sem=send_sem,
            recv_sem=recv_sem,
            device_id={axis: peer},
            device_id_type=MESH,
        )

    def whole1(part):
        rest = pl.ds(0, SPACE - 1)
        return whole(
            sbuf.at[part, rest], rbuf.at[part, rest], p1_ssem.at[part], p1_rsem.at[part], "space", upper
        )

    def whole2(part):
        rest = pl.ds(0, SPACE - 1)
        return whole(
            sbuf2.at[part, rest], rbuf2.at[part, rest], p2_ssem.at[part], p2_rsem.at[part], "space", upper
        )

    fill(0)
    pl.semaphore_wait(barrier, SPACE - 1 + EVENTS - 1)
    start_all(phase1(0))

    for fetch in fetches[2:]:
        fetch.wait()
    hf = hf_in[...]
    hf_row = jnp.concatenate([hf[0:1], hf[1:2]], axis=1)
    can[...] = onehot(iota((ELEMS, ELEMS), 0) == hf_row)
    even = jnp.bitwise_and(iota((1, 8, 128), 1), 1) == 0
    field = lax.shift_right_logical(iota((1, 8, 128), 1), 1)
    height = jnp.bitwise_and(iota((1, 8, 128), 2), 15)

    wide = iota((512, ELEMS), 0)
    spread[...] = onehot(
        iota((512, ELEMS), 1)
        == jnp.bitwise_and(lax.shift_right_logical(wide, 1), 3) * 64
        + lax.shift_right_logical(wide, 3)
    )
    spread_one = onehot(iota((512, 64), 1) == lax.shift_right_logical(iota((512, 64), 0), 3))

    def by_layer(rows):
        return jnp.where(
            even, rows[:, 0:128].reshape(64, 8, 128), rows[:, 128:256].reshape(64, 8, 128)
        )

    def to_slab(x, spreading):
        result = None
        for part in split3(x):
            moved = nn(spreading, nn(part, can[...]).astype(BF16))
            result = moved if result is None else result + moved
        return by_layer(result).reshape(4, 4, 4, 8, 128)

    states[0] = to_slab(y_in[...], spread[...])
    cc[...] = to_slab(c_in[...], spread_one)
    w1[...] = to_slab(w_in[0:64, :], spread_one)
    w2[...] = to_slab(w_in[64:128, :], spread_one)
    for side, (position, sign) in enumerate(((0, 1.0), (3, -1.0))):
        speed = cc[position]
        wind = sign * w1[position]
        pe[side] = 3.0 * (wind - (speed + jnp.abs(wind)))
        speed = cc[:, position]
        wind = sign * w2[:, position]
        pn[side] = 3.0 * (wind - (speed + jnp.abs(wind)))
        pu[side] = -3.0 * cc[:, :, position]
    cc[...] = jnp.where(field == 0, cc[...] * cc[...], 1.0)
    target = es_in[0] - me * ELEMS
    at_source = (jnp.concatenate([hf, hf, hf, hf], axis=0) == target).reshape(1, 8, 128)
    at_source = jnp.logical_and(at_source, field == 0)[0]

    def place_source(n, carry):
        src[n] = jnp.where(at_source, wave_in[0, n], 0.0)
        return carry

    lax.fori_loop(0, 64, place_source, 0)

    def halo_up(i):
        return pltpu.make_async_remote_copy(
            src_ref=halo_send.at[i, 1],
            dst_ref=halo_recv.at[i, 0],
            send_sem=halo_ssem.at[i, 1],
            recv_sem=halo_rsem.at[i, 0],
            device_id={"space": upper},
            device_id_type=MESH,
        )

    def halo_down(i):
        return pltpu.make_async_remote_copy(
            src_ref=halo_send.at[i, 0],
            dst_ref=halo_recv.at[i, 1],
            send_sem=halo_ssem.at[i, 0],
            recv_sem=halo_rsem.at[i, 1],
            device_id={"space": lower},
            device_id_type=MESH,
        )

    def send_halo(i):
        first = states[i, 0].reshape(16, 8, 128)
        last = states[i, 3].reshape(16, 8, 128)
        halo_send[i, 1] = (
            jnp.where(even, roll(last[8:16], 7, 1), last[0:8]).reshape(4, 16, 128).astype(BF16)
        )
        halo_send[i, 0] = (
            jnp.where(even, first[0:8], roll(first[8:16], 1, 1)).reshape(4, 16, 128).astype(BF16)
        )
        halo_up(i).start()
        halo_down(i).start()

    def section(i):
        y = states.at[i]
        first = y[0].reshape(16, 8, 128)
        last = y[3].reshape(16, 8, 128)
        for k in range(4):
            ge[k] = line(TABLE[k], lambda j: y[j])
            gn[:, k] = line(TABLE[k], lambda j: y[:, j])
            gu[:, :, k] = line(TABLE[k], lambda j: y[:, :, j])
        tend[...] = w1[...] * ge[...] + w2[...] * gn[...] + src[...].reshape(4, 4, 4, 8, 128)
        for side, (here, there, shift, sign) in enumerate(((0, 3, 16, 3.0), (3, 0, 112, -3.0))):
            outside = roll(y[:, there].reshape(16, 8, 128), shift, 2).reshape(4, 4, 8, 128)
            jump = y[:, here] - outside
            tend[:, here] += pn[side] * jump
            gn[:, here] += sign * jump
        for side, (here, there, shift, sign, wall) in enumerate(
            ((0, 3, 1, 3.0, 0), (3, 0, 127, -3.0, 15))
        ):
            outside = roll(y[:, :, there].reshape(16, 8, 128), shift, 2)
            outside = jnp.where(height == wall, 0.0, outside).reshape(4, 4, 8, 128)
            jump = y[:, :, here] - outside
            tend[:, :, here] += pu[side] * jump
            gu[:, :, here] += sign * jump
        halo_up(i).wait_recv()
        halo_down(i).wait_recv()
        arrived = halo_recv[i, 0].astype(F32).reshape(8, 8, 128)
        arrived = jnp.concatenate([roll(arrived, 7, 1), arrived], axis=0)
        outside = jnp.where(even, arrived, roll(last, 1, 1)).reshape(4, 4, 8, 128)
        jump = y[0] - outside
        tend[0] += pe[0] * jump
        ge[0] += 3.0 * jump
        arrived = halo_recv[i, 1].astype(F32).reshape(8, 8, 128)
        arrived = jnp.concatenate([roll(arrived, 1, 1), arrived], axis=0)
        outside = jnp.where(even, roll(first, 7, 1), arrived).reshape(4, 4, 8, 128)
        jump = y[3] - outside
        tend[3] += pe[1] * jump
        ge[3] += -3.0 * jump
        for a in range(4):
            east = ge[a].reshape(16, 8, 128)
            north = gn[a].reshape(16, 8, 128)
            up = gu[a].reshape(16, 8, 128)
            swapped = (
                roll(jnp.where(field == 0, east, jnp.where(field == 3, up, 0.0)), 2, 1)
                + roll(jnp.where(field == 1, east, jnp.where(field == 0, up, 0.0)), 6, 1)
                + roll(jnp.where(jnp.bitwise_and(field, 1) == 0, north, 0.0), 4, 1)
            )
            slope = tend[a] - cc[a] * swapped.reshape(4, 4, 8, 128)
            if i == 0:
                total[a] = slope
            elif i < 3:
                total[a] += 2.0 * slope
            else:
                total[a] = states[0, a] + (TIME_STEP / 6.0) * (total[a] + slope)
            if i < 3:
                states[i + 1, a] = states[0, a] + (TIME_STEP if i == 2 else TIME_STEP / 2) * slope

    k8 = iota((8, SPACE), 0) * 32 + me
    off8 = jnp.sum(jnp.where(end_row.astype(I32) <= k8, 1.0, 0.0), axis=1, keepdims=True)
    off = jnp.broadcast_to(off8.astype(I32).reshape(1, 8, 1), (64, 8, 1)).reshape(512, 1)
    row = iota((512, 1), 0)
    origin = (
        jnp.bitwise_and(lax.shift_right_logical(row, 4) - off + SPACE, SPACE - 1) * 16
        + jnp.bitwise_and(row, 15)
    )

    def relay(part):
        whole1(part).wait_recv()
        rows = nn(onward[...], rbuf[part].reshape(512, 256)).astype(BF16)
        sbuf2[part] = rows.reshape(SPACE, 16, 256)
        rbuf2[part, me] = sbuf2[part, me]
        start_all(phase2(part))

    send_halo(0)
    fill(1)
    start_all(phase1(1))
    onward[...] = onehot(iota((512, 512), 1) == origin)
    section(0)
    send_halo(1)
    relay(0)
    section(1)
    send_halo(2)
    relay(1)
    section(2)
    send_halo(3)

    def rows_from_slab(parts, selectors):
        result = None
        for part in parts:
            pieces = [nn(selector, part).astype(BF16) for selector in selectors]
            moved = nt(jnp.concatenate(pieces, axis=1), can[...])
            result = moved if result is None else result + moved
        return result

    shape = (ELEMS, 512)
    wanted_row = (
        jnp.bitwise_and(iota(shape, 0), 63) * 8 + lax.shift_right_logical(iota(shape, 0), 6) * 2
    )
    gather_rows = [onehot(iota(shape, 1) == wanted_row + layer) for layer in range(2)]
    landing = rs_in[...]
    places = iota((SPACE, 512), 1)
    landed = jnp.zeros((SPACE, 512), F32)
    for r in range(SPACE):
        label = start_back.astype(I32) + r
        place = jnp.bitwise_and(label, 31) * 16 + lax.shift_right_logical(label, 5)
        column = landing[:, r : r + 1]
        hit = jnp.logical_and(places == place, column < ELEMS)
        landed = landed + jnp.where(hit, column.astype(F32) + 1.0, 0.0)
    land_row = jnp.sum(landed, axis=0, keepdims=True) - 1.0
    land_row = jnp.broadcast_to(land_row, (8, 512))
    eye = onehot(iota((ELEMS, ELEMS), 0) == iota((ELEMS, ELEMS), 1))
    hf_col = nt(eye, jnp.broadcast_to(hf_row, (8, ELEMS)).astype(F32).astype(BF16))[:, 0:1]

    for h in range(2):
        place_row = (land_row if h == 0 else roll(land_row, 8, 1))[0:1]
        settle[h] = onehot(hf_col == place_row)

    weights = [TIME_STEP / 6.0, TIME_STEP / 3.0, TIME_STEP / 3.0, TIME_STEP / 6.0]
    for part in range(2):
        for h in range(2):
            i = 2 * h + part
            y = weights[i] * states[i].reshape(64, 8, 128)
            own = jnp.where(field == 0, y, 0.0)
            own = own + roll(own, 4, 1)
            weighted[h] = y
            pressure[h] = own + roll(own, 2, 1)
        whole2(part).wait_recv()
        for h in range(2):
            settled = nn(settle[h], rbuf2[part].reshape(512, 256)).astype(BF16)
            qa[h] = by_layer(nt(spread[...], settled)).reshape(4, 4, 4, 8, 128)
        for a in range(4):
            east = north = speed = None
            for h in range(2):
                q = qa.at[h]
                d_east = line(TABLE_LOW[a], lambda j: q[j]).reshape(16, 8, 128)
                d_north = jnp.stack(
                    [line(TABLE_LOW[k], lambda j: q[a, j]) for k in range(4)], axis=0
                ).reshape(16, 8, 128)
                d_up = jnp.stack(
                    [line(TABLE_LOW[k], lambda j: q[a, :, j]) for k in range(4)], axis=1
                ).reshape(16, 8, 128)
                y = weighted[h, a * 16 : (a + 1) * 16]
                own = pressure[h, a * 16 : (a + 1) * 16]
                product = own * jnp.where(
                    field == 1,
                    d_east,
                    jnp.where(field == 2, d_north, jnp.where(field == 3, d_up, 0.0)),
                )
                east = y * d_east if east is None else east + y * d_east
                north = y * d_north if north is None else north + y * d_north
                speed = product if speed is None else speed + product
            rows = slice(a * 16, (a + 1) * 16)
            if part == 0:
                acc[0, rows] = speed
                acc[1, rows] = east
                acc[2, rows] = north
            else:
                acc[0, rows] += speed
                acc[1, rows] += east
                acc[2, rows] += north
    for g in range(3):
        sums = acc[g] + roll(acc[g], 4, 1)
        sums = (sums + roll(sums, 2, 1)).reshape(16, 4, 8, 128)
        packed = jnp.where(
            field == 0,
            sums[:, 0],
            jnp.where(field == 1, sums[:, 1], jnp.where(field == 2, sums[:, 2], sums[:, 3])),
        )
        gsend[:, g] = (-packed).reshape(EVENTS, 2, 8, 128)

    def scatter(d):
        peer = lax.rem(ev + d, EVENTS)
        return pltpu.make_async_remote_copy(
            src_ref=gsend.at[peer],
            dst_ref=grecv.at[ev],
            send_sem=rs_ssem.at[0],
            recv_sem=rs_rsem.at[0],
            device_id={"event": peer},
            device_id_type=MESH,
        )

    def gather(d):
        peer = lax.rem(ev + d, EVENTS)
        return pltpu.make_async_remote_copy(
            src_ref=gown,
            dst_ref=out_g.at[ev],
            send_sem=ag_ssem.at[0],
            recv_sem=ag_rsem.at[0],
            device_id={"event": peer},
            device_id_type=MESH,
        )

    grecv[ev] = gsend[ev]
    for d in (4, 5, 3, 2, 6, 7, 1):
        scatter(d).start()
    rest = pl.ds(0, EVENTS - 1)
    next_event = lax.rem(ev + 1, EVENTS)
    scattered = whole(
        gsend.at[rest], grecv.at[rest], rs_ssem.at[0], rs_rsem.at[0], "event", next_event
    )
    gathered = whole(
        gsend.at[rest], out_g.at[rest], ag_ssem.at[0], ag_rsem.at[0], "event", next_event
    )
    section(3)
    end[...] = rows_from_slab(split3(total[...].reshape(512, 128)), gather_rows).reshape(
        4, 64, ELEMS
    )
    to_hbm = pltpu.make_async_copy(end, out_y, out_sem.at[0])
    to_hbm.start()
    for part in range(2):
        whole1(part).wait_send()
        whole2(part).wait_send()
    for i in range(4):
        halo_up(i).wait_send()
        halo_down(i).wait_send()
    shape = (24, 48)
    node = jnp.bitwise_and(iota(shape, 0), 7)
    position = (
        lax.shift_right_logical(iota(shape, 0), 3) * 16
        + lax.shift_right_logical(node, 2) * 8
        + jnp.bitwise_and(node, 3) * 2
    )
    gather_rows = [onehot(iota(shape, 1) == position + layer) for layer in range(2)]
    scattered.wait_recv()
    summed = grecv[0]
    for e in range(1, EVENTS):
        summed = summed + grecv[e]
    rows = rows_from_slab(split3(summed.reshape(48, 128)), gather_rows)
    speed = c_in[pl.ds(pl.multiple_of(ev * 8, 8), 8), :]
    gown[...] = jnp.concatenate([2.0 * speed * rows[0:8], rows[8:24]], axis=0).reshape(3, 8, ELEMS)
    own = pltpu.make_async_copy(gown, out_g.at[ev], out_sem.at[1])
    own.start()
    for d in (4, 5, 3, 2, 6, 7, 1):
        gather(d).start()
    scattered.wait_send()
    gathered.wait_recv()
    gathered.wait_send()
    own.wait()
    to_hbm.wait()


def deliver(y_hbm, g_hbm, out_y, out_s, out_w, y, g, sem):
    steps = [(y_hbm.at[f], y.at[f], out_y.at[f]) for f in range(4)]
    steps += [(g_hbm.at[:, 0], g.at[0], out_s)]
    steps += [(g_hbm.at[:, 1 + d], g.at[1 + d], out_w.at[d]) for d in range(2)]
    arrive = [pltpu.make_async_copy(a, b, sem.at[0, k]) for k, (a, b, _) in enumerate(steps)]
    leave = [pltpu.make_async_copy(b, c, sem.at[1, k]) for k, (_, b, c) in enumerate(steps)]
    for copy in arrive:
        copy.start()
    for first, second in zip(arrive, leave):
        first.wait()
        second.start()
    for copy in leave:
        copy.wait()


def shards(
    adjoint_start,
    checkpoints,
    sound_speed,
    wind_field,
    neighbours,
    halo_faces,
    send_list,
    recv_slots,
    event_source,
    source_wave,
):
    del neighbours
    anywhere = pl.BlockSpec(memory_space=pl.ANY)
    nodes = (4, 4, 4, 8, 128)
    dma = pltpu.SemaphoreType.DMA
    end, gradients = pl.pallas_call(
        kernel,
        out_shape=(
            jax.ShapeDtypeStruct((4, 64, ELEMS), F32),
            jax.ShapeDtypeStruct((EVENTS, 3, 8, ELEMS), F32),
        ),
        in_specs=[anywhere] * 9,
        out_specs=(anywhere, anywhere),
        scratch_shapes=[
            pltpu.VMEM((ELEMS, ELEMS), F32),
            pltpu.VMEM((1024, ELEMS), BF16),
            pltpu.VMEM((64, ELEMS), F32),
            pltpu.VMEM((128, ELEMS), F32),
            pltpu.VMEM((2, 128), I32),
            pltpu.VMEM((SPACE, SPACE), I32),
            pltpu.VMEM((SPACE, SPACE), I32),
            pltpu.SMEM((1,), I32),
            pltpu.SMEM((1, 64), F32),
            pltpu.VMEM((4,) + nodes, F32),
            pltpu.VMEM(nodes, F32),
            pltpu.VMEM(nodes, F32),
            pltpu.VMEM(nodes, F32),
            pltpu.VMEM(nodes, F32),
            pltpu.VMEM(nodes, F32),
            pltpu.VMEM(nodes, F32),
            pltpu.VMEM(nodes, F32),
            pltpu.VMEM(nodes, F32),
            pltpu.VMEM((2, 4, 4, 8, 128), F32),
            pltpu.VMEM((2, 4, 4, 8, 128), F32),
            pltpu.VMEM((2, 4, 4, 8, 128), F32),
            pltpu.VMEM((64, 8, 128), F32),
            pltpu.VMEM((ELEMS, ELEMS), BF16),
            pltpu.VMEM((512, ELEMS), BF16),
            pltpu.VMEM((512, 512), BF16),
            pltpu.VMEM((2, ELEMS, 512), BF16),
            pltpu.VMEM((4, 2, 4, 16, 128), BF16),
            pltpu.VMEM((4, 2, 4, 16, 128), BF16),
            pltpu.VMEM((2, SPACE, 16, 256), BF16),
            pltpu.VMEM((2, SPACE, 16, 256), BF16),
            pltpu.VMEM((2, SPACE, 16, 256), BF16),
            pltpu.VMEM((2, SPACE, 16, 256), BF16),
            pltpu.VMEM((2,) + nodes, F32),
            pltpu.VMEM((2, 64, 8, 128), F32),
            pltpu.VMEM((2, 64, 8, 128), F32),
            pltpu.VMEM((3, 64, 8, 128), F32),
            pltpu.VMEM((EVENTS, 3, 2, 8, 128), F32),
            pltpu.VMEM((EVENTS, 3, 2, 8, 128), F32),
            pltpu.VMEM((3, 8, ELEMS), F32),
            pltpu.VMEM((4, 64, ELEMS), F32),
            dma((9,)),
            dma((4, 2)),
            dma((4, 2)),
            dma((2,)),
            dma((2,)),
            dma((2,)),
            dma((2,)),
            dma((1,)),
            dma((1,)),
            dma((1,)),
            dma((1,)),
            dma((2,)),
        ],
        compiler_params=pltpu.CompilerParams(
            collective_id=0, has_side_effects=True
        ),
        name="adjoint_step",
    )(
        adjoint_start.reshape(ELEMS, ELEMS),
        checkpoints.reshape(1024, ELEMS),
        sound_speed,
        wind_field.reshape(128, ELEMS),
        halo_faces,
        send_list,
        recv_slots,
        event_source,
        source_wave,
    )
    end, speed, wind = pl.pallas_call(
        deliver,
        out_shape=(
            jax.ShapeDtypeStruct((4, 64, ELEMS), F32),
            jax.ShapeDtypeStruct((EVENTS, 8, ELEMS), F32),
            jax.ShapeDtypeStruct((2, EVENTS, 8, ELEMS), F32),
        ),
        in_specs=[anywhere] * 2,
        out_specs=(anywhere,) * 3,
        scratch_shapes=[
            pltpu.VMEM((4, 64, ELEMS), F32),
            pltpu.VMEM((3, EVENTS, 8, ELEMS), F32),
            dma((2, 7)),
        ],
        name="deliver",
    )(end, gradients)
    return (
        end.reshape(1, 4, 64, ELEMS),
        speed.reshape(64, ELEMS),
        wind.reshape(2, 64, ELEMS),
    )


def solution(mesh):
    return jax.shard_map(
        shards,
        mesh=mesh,
        in_specs=(
            P("event", None, None, "space"),
            P("event", None, None, None, "space"),
            P(None, "space"),
            P(None, None, "space"),
            P(None, "space"),
            P(None, "space"),
            P("space", None),
            P("space", None),
            P("event"),
            P("event", None),
        ),
        out_specs=(P("event", None, None, "space"), P(None, "space"), P(None, None, "space")),
        check_vma=False,
    )
```
